128 devices in a mesh: pencil: 128 (over x, y, z, core).
Axes of the slice: x: 4, y: 4, z: 4, core: 2. Of those that a mesh axis runs over, the one named last changes fastest.
Arguments:
- coefficients: float32 [2, 8, 16384, 128], P(None, None, 'pencil'), may hold values from -6 to 6
- potential: float32 [256, 256, 256], P('pencil'), may hold values from -5 to 5
- slot_atom: int32 [8192], P('pencil'), may hold values from 0 to 2047, as said below
- slot_count: int32 [128], P('pencil'), may hold values from 8 to 64, as said below
- point_offset: int32 [8192, 256], P('pencil'), may hold values from 0 to 131071
- proj_value: float32 [8192, 8, 256], P('pencil'), may hold values from -0.7 to 0.7
- proj_strength: float32 [2048, 8], replicated, may hold values from 0.5 to 4
- proj_count: int32 [2048], replicated, may hold values from 1 to 8
Outputs:
- applied_coefficients: float32 [2, 8, 16384, 128], P(None, None, 'pencil')
- projections: float32 [2048, 128], P('pencil')
The draws below stay inside these ranges and needn't reach their ends.
Inputs may be any that keep to these rules, and one draw needn't show every extreme that they name: `slot_atom`: the home block of atom a is a // 16; the atom of every slot of block d has its home block within 2 of d modulo the number of blocks, so (a // 16 - d) modulo the number of blocks is at most 2 or at least the number of blocks minus 2. `slot_count`: some block uses all 64 slots.
All inputs are finite; a program needn't handle non-finite values.
Results may differ from the reference program's by a relative error of at most 0.00011.
Values sent between devices are 32-bit elements; how exact they have to be, the bound alone decides.
No kernel may reach another device: no remote copies, remote signals or barrier semaphores. Data moves between devices by JAX's collectives and lax.ppermute only.
A program may use at most 256 MiB of HBM per device.

```python
import math
import jax
import jax.numpy as jnp
from jax import lax

GRID_SIDE = 256
WAVE_CUTOFF = 128
ZL = 2
BANDS = 8
ATOM_DEV = 16
ATOMS = 2048
NPROJ = 8
SLOTS = 64
NPTS = 256
REACH = 2
N_PENCIL = 128


def draw_slot_atom(key, part):
    key_reach = jax.random.fold_in(key, 11)
    key_within = jax.random.fold_in(key, 12)
    count_all = N_PENCIL * SLOTS
    blocks = jnp.arange(count_all, dtype=jnp.int32) // SLOTS
    offsets = jax.random.randint(key_reach, (count_all,), -REACH, REACH + 1, dtype=jnp.int32)
    within = jax.random.randint(key_within, (count_all,), 0, ATOM_DEV, dtype=jnp.int32)
    offsets = offsets.at[0].set(0).at[count_all - 1].set(0)
    within = within.at[0].set(0).at[count_all - 1].set(ATOM_DEV - 1)
    home_block = (blocks + offsets) % N_PENCIL
    return (home_block * ATOM_DEV + within).astype(jnp.int32)


def draw_slot_count(key, part):
    key_base = jax.random.fold_in(key, 21)
    key_heavy = jax.random.fold_in(key, 22)
    key_pick = jax.random.fold_in(key, 23)
    base_count = jax.random.randint(key_base, (N_PENCIL,), SLOTS // 8, SLOTS // 2 + 1, dtype=jnp.int32)
    heavy_block = jax.random.randint(key_heavy, (N_PENCIL,), 0, 16, dtype=jnp.int32) == 0
    counts = jnp.where(heavy_block, SLOTS, base_count)
    chosen = jax.random.randint(key_pick, (), 0, N_PENCIL, dtype=jnp.int32)
    counts = counts.at[chosen].set(SLOTS).at[(chosen + 1) % N_PENCIL].set(SLOTS // 8)
    return counts.astype(jnp.int32)


def set_ends(entries, key, low, high):
    extent = entries.shape
    index_at = [jax.random.randint(jax.random.fold_in(key, axis), (), 0, extent[axis]) for axis in range(len(extent))]
    entries = entries.at[tuple(index_at)].set(low)
    longest = extent.index(max(extent))
    index_at[longest] = (index_at[longest] + 1) % extent[longest]
    return entries.at[tuple(index_at)].set(high)


def block_scale(rng, extent, pieces, low, largest):
    factor_of = 1.0
    for position, blocks in pieces:
        heights = jax.random.uniform(jax.random.fold_in(jax.random.fold_in(rng, 6), position), (blocks,), jnp.float32, low / len(pieces), largest / len(pieces))
        factor_of = factor_of * jnp.repeat(jnp.exp(heights), extent[position] // blocks).reshape((-1,) + (1,) * (len(extent) - 1 - position))
    return factor_of


def gaussian(stream_key, shape, deviation, reach, split=(), kind=jnp.bfloat16):
    factor_of = block_scale(stream_key, shape, split, -0.22, 0.18) if split else 1.0
    entries = jax.random.normal(stream_key, shape, jnp.float32) * deviation * factor_of
    return jnp.minimum(jnp.maximum(entries, -reach), reach).astype(kind)


def setup_inputs(seed: int = 0) -> dict:
    key_of = jax.random.split(jax.random.key(seed), 9)
    return {
        "coefficients": gaussian(key_of[0], (2, BANDS, WAVE_CUTOFF * WAVE_CUTOFF, WAVE_CUTOFF), 1.0, 6.0, ((2, 128),), jnp.float32),
        "potential": gaussian(key_of[1], (GRID_SIDE, GRID_SIDE, GRID_SIDE), 1.0, 5.0, ((0, 128),), jnp.float32),
        "slot_atom": draw_slot_atom(jax.random.fold_in(key_of[8], 71), 0),
        "slot_count": draw_slot_count(jax.random.fold_in(key_of[8], 71), 0),
        "point_offset": set_ends(jax.random.randint(key_of[4], (N_PENCIL * SLOTS, NPTS), 0, ZL * GRID_SIDE * GRID_SIDE), jax.random.fold_in(key_of[4], 1), 0, (ZL * GRID_SIDE * GRID_SIDE) - 1).astype(jnp.int32),
        "proj_value": gaussian(key_of[5], (N_PENCIL * SLOTS, NPROJ, NPTS), 0.12, 0.7, ((0, 128),), jnp.float32),
        "proj_strength": jnp.clip(jnp.exp(jax.random.uniform(key_of[6], (ATOMS, NPROJ), jnp.float32, math.log(0.5), math.log(4.0))), 0.5, 4.0),
        "proj_count": set_ends(jax.random.randint(key_of[7], (ATOMS,), 1, NPROJ + 1), jax.random.fold_in(key_of[7], 1), 1, NPROJ).astype(jnp.int32),
    }


def kinetic_table():
    frequency = jnp.arange(WAVE_CUTOFF, dtype=jnp.int32) - WAVE_CUTOFF // 2
    squared = (frequency * frequency).astype(jnp.float32)
    summed = squared[:, None, None] + squared[None, :, None] + squared[None, None, :]
    return (6.0 / (WAVE_CUTOFF * WAVE_CUTOFF)) * summed.reshape(WAVE_CUTOFF * WAVE_CUTOFF, WAVE_CUTOFF)


def reference(coefficients, potential, slot_atom, slot_count, point_offset, proj_value, proj_strength, proj_count):
    highest = lax.Precision.HIGHEST
    box_index = (jnp.arange(WAVE_CUTOFF, dtype=jnp.int32) - WAVE_CUTOFF // 2) % GRID_SIDE
    slot_all = N_PENCIL * SLOTS
    slot_block = jnp.arange(slot_all, dtype=jnp.int32) // SLOTS
    used_slot = (jnp.arange(slot_all, dtype=jnp.int32) % SLOTS) < slot_count[slot_block]
    cell_index = (slot_block[:, None] * (ZL * GRID_SIDE * GRID_SIDE) + point_offset).astype(jnp.int32)
    weights = jnp.where(used_slot[:, None, None], proj_value, jnp.zeros_like(proj_value))
    proj_mask = jnp.arange(NPROJ, dtype=jnp.int32)[None, :] < proj_count[:, None]
    slot_strength = proj_strength[slot_atom]
    kinetic = kinetic_table()
    potential_flat = potential.reshape(-1)

    def one_band(band_amplitudes):
        grid_real = jnp.zeros((GRID_SIDE, GRID_SIDE, GRID_SIDE), jnp.float32).at[box_index[:, None, None], box_index[None, :, None], box_index[None, None, :]].set(band_amplitudes[0].reshape(WAVE_CUTOFF, WAVE_CUTOFF, WAVE_CUTOFF))
        grid_imag = jnp.zeros((GRID_SIDE, GRID_SIDE, GRID_SIDE), jnp.float32).at[box_index[:, None, None], box_index[None, :, None], box_index[None, None, :]].set(band_amplitudes[1].reshape(WAVE_CUTOFF, WAVE_CUTOFF, WAVE_CUTOFF))
        field_grid = jnp.fft.ifftn(lax.complex(grid_real, grid_imag)) * ((GRID_SIDE ** 3) * (WAVE_CUTOFF ** -1.5))
        ordered = jnp.transpose(field_grid, (2, 1, 0)).reshape(-1)
        fields = jnp.stack([jnp.real(ordered), jnp.imag(ordered)])
        picked = fields[:, cell_index]
        partial_terms = jnp.einsum('cst,spt->scp', picked, weights, precision=highest)
        summed = jax.ops.segment_sum(partial_terms, slot_atom, num_segments=ATOMS)
        becp_band = jnp.where(proj_mask[:, None, :], summed, jnp.zeros_like(summed))
        energy = becp_band[slot_atom] * slot_strength[:, None, :]
        added = jnp.einsum('scp,spt->cst', energy, weights, precision=highest)
        projected = jnp.zeros_like(fields).at[:, cell_index].add(added)
        applied = potential_flat[None, :] * fields + projected
        grid_back = jnp.transpose(lax.complex(applied[0], applied[1]).reshape(GRID_SIDE, GRID_SIDE, GRID_SIDE), (2, 1, 0))
        spectrum = jnp.fft.fftn(grid_back) * (GRID_SIDE ** -1.5)
        kept = spectrum[box_index][:, box_index][:, :, box_index].reshape(WAVE_CUTOFF * WAVE_CUTOFF, WAVE_CUTOFF)
        result = jnp.stack([jnp.real(kept), jnp.imag(kept)]) + kinetic[None] * band_amplitudes
        return result, becp_band

    results, becps = lax.map(one_band, jnp.transpose(coefficients, (1, 0, 2, 3)))
    applied_coefficients = jnp.transpose(results, (1, 0, 2, 3))
    projections = jnp.transpose(becps, (1, 2, 0, 3)).reshape(ATOMS, 2 * BANDS * NPROJ)
    return applied_coefficients, projections
```

```python
import jax
import jax.numpy as jnp
import ml_dtypes
import numpy as np
from jax import lax
from jax.experimental import pallas as pl
from jax.experimental.pallas import tpu as pltpu
from jax.sharding import PartitionSpec as P

GRID = 256
CUT = 128
NPROJ = 8
REACH = 2
BANDS = 8
SLOTS = 64
NPTS = 256
ROWS = 16384
WINDOW = 2 * REACH + 1
F32 = jnp.float32
BF16 = jnp.bfloat16
VMEM_LIMIT = 56 * 1024 * 1024


def halves(table):
    table = np.asarray(table, np.float64)
    high = table.astype(np.float32).astype(ml_dtypes.bfloat16)
    low = (table - high.astype(np.float64)).astype(np.float32).astype(ml_dtypes.bfloat16)
    return high, low


def make_tables():
    freq = np.arange(CUT) - CUT // 2
    turns = (freq[:, None] * np.arange(GRID)[None, :]) % GRID
    cos = np.cos(2 * np.pi * turns / GRID)
    sin = np.sin(2 * np.pi * turns / GRID)
    up = CUT ** -0.5
    down = GRID ** -0.5
    planes = np.concatenate([np.arange(0, GRID, 2), np.arange(1, GRID, 2)])
    cz, sz = cos[:, planes], sin[:, planes]
    fz = up * np.block([[cz.T, -sz.T], [sz.T, cz.T]])
    fy = up * np.block([[cos, sin], [-sin, cos]])
    fx = up * np.concatenate([cos.T, sin.T], 1)
    bx = down * np.concatenate([cos, sin], 0)
    by = down * np.block([[cos.T, -sin.T], [sin.T, cos.T]])
    bz = down * np.block([[cz.T, -sz.T], [sz.T, cz.T]])
    return {k: halves(v) for k, v in dict(fz=fz, fy=fy, fx=fx, bx=bx, by=by, bz=bz).items()}


TABLES = make_tables()


def split(value):
    high = value.astype(BF16)
    low = (value - high.astype(F32)).astype(BF16)
    return high, low


def mm(a, b):
    return lax.dot_general(a, b, (((1,), (0,)), ((), ())), preferred_element_type=F32)


def mm_nt(a, b):
    return lax.dot_general(a, b, (((1,), (1,)), ((), ())), preferred_element_type=F32)


def mm_tn(a, b):
    return lax.dot_general(a, b, (((0,), (0,)), ((), ())), preferred_element_type=F32)


def lane_iota(shape):
    return lax.broadcasted_iota(jnp.int32, shape, len(shape) - 1)


def exchange_blocks(arrays):
    rows = arrays[0].shape[0]
    block = lane_iota((rows, 128)) // 8
    rolled = [pltpu.roll(a, 8 * i, 1) if i else a for i, a in enumerate(arrays)]
    vals = [rolled[(-n) % 16] for n in range(16)]
    for bit in range(4):
        step = 1 << bit
        chosen = (block // step) % 2 == 1
        vals = [jnp.where(chosen, vals[(j - step) % 16], vals[j]) for j in range(16)]
    return [pltpu.roll(v, (128 - 8 * j) % 128, 1) if j else v for j, v in enumerate(vals)]


def swap_parts(value, first_sign):
    rolled = pltpu.roll(value, 64, 1)
    first = lane_iota(value.shape) < 64
    return jnp.where(first, first_sign * rolled, -first_sign * rolled)


def block_ones():
    row = lax.broadcasted_iota(jnp.int32, (128, 128), 0) // 8
    col = lax.broadcasted_iota(jnp.int32, (128, 128), 1) // 8
    return (row == col).astype(F32)


def three(value):
    a = value.astype(BF16)
    rest = value - a.astype(F32)
    b = rest.astype(BF16)
    c = (rest - b.astype(F32)).astype(BF16)
    return a, b, c


def exact_times_ones(value, ones):
    ones = ones.astype(BF16)
    a, b, c = three(value)
    return mm(a, ones) + mm(b, ones) + mm(c, ones)


def slot_weights(values, groups):
    return jnp.concatenate([jnp.where(groups == g, values, 0.0) for g in range(8)], 0)


def columns_kernel(coef_ref, th_ref, tl_ref, out_ref):
    th, tl = th_ref[...], tl_ref[...]
    for b in range(BANDS):
        a = jnp.concatenate([coef_ref[0, b], coef_ref[1, b]], 1)
        ah, al = split(a)
        res = mm_nt(th, ah) + mm_nt(tl, ah) + mm_nt(th, al)
        for q in range(4):
            out_ref[pl.ds(q * 8 + b, 128, stride=32), :] = res[q * 128:(q + 1) * 128]


def grid_kernel(
    rows_sm, count_sm,
    recv_ref, pot_ref, value_ref, group_ref, window_ref,
    yh_ref, yl_ref, xh_ref, xl_ref,
    field_hbm, partial_ref,
    ah_s, al_s, ys_s, inh_s, inl_s, u_s, w_s, gat_s, z_s, sem,
):
    yh, yl = yh_ref[...], yl_ref[...]
    piece = lax.broadcasted_iota(jnp.int32, (32, 128), 0)
    pick_group = (lane_iota((32, 128)) % 8 == piece % 8).astype(F32).astype(BF16)
    for zz in range(2):
        for b in range(BANDS):
            for r in range(2):
                part = recv_ref[pl.ds(r * 16 + zz * 8 + b, 128, stride=32), :]
                h, l = split(part)
                ah_s[b * 128:(b + 1) * 128, r * 128:(r + 1) * 128] = h
                al_s[b * 128:(b + 1) * 128, r * 128:(r + 1) * 128] = l
        ah, al = ah_s[...], al_s[...]
        ys_s[...] = mm(ah, yh) + mm(al, yh) + mm(ah, yl)
        for half in range(2):
            def permute(kc, carry, half=half):
                base = pl.multiple_of(kc * 16, 16)
                ins = [
                    ys_s[pl.ds((i % 8) * 128 + base, 16), ((i // 8) * 2 + half) * 128:((i // 8) * 2 + half + 1) * 128]
                    for i in range(16)
                ]
                outs = exchange_blocks(ins)
                for j, v in enumerate(outs):
                    s = swap_parts(v, -1.0)
                    pair = half * 8 + j // 2
                    cols = slice((j % 2) * 128, (j % 2 + 1) * 128)
                    vh, vl = split(v)
                    sh, sl = split(s)
                    inh_s[pair, pl.ds(base, 16), cols] = vh
                    inl_s[pair, pl.ds(base, 16), cols] = vl
                    inh_s[pair, pl.ds(128 + base, 16), cols] = sh
                    inl_s[pair, pl.ds(128 + base, 16), cols] = sl
                return carry

            lax.fori_loop(0, 8, permute, 0)

        def along_x(pair, carry, zz=zz):
            xh, xl = xh_ref[...], xl_ref[...]
            bh, bl = inh_s[pair], inl_s[pair]
            res = mm(xh, bh) + mm(xl, bh) + mm(xh, bl)
            for k in range(2):
                yg = pair * 2 + k
                pot = pot_ref[zz, pl.ds(pl.multiple_of(yg * 8, 8), 8), :]
                pa, pb, pc = three(pot)
                pieces = jnp.concatenate([pa.astype(F32), pb.astype(F32), pc.astype(F32), jnp.zeros((8, 256), F32)], 0)
                spread = mm_tn(pieces.astype(BF16), pick_group)
                u = res[:, k * 128:(k + 1) * 128]
                at = pl.multiple_of((zz * 32 + yg) * 256, 256)
                u_s[pl.ds(at, 256), :] = u
                w_s[pl.ds(at, 256), :] = u * spread
            return carry

        lax.fori_loop(0, 16, along_x, 0)
    out_copy = pltpu.make_async_copy(w_s, field_hbm, sem)
    out_copy.start()

    z_s[...] = jnp.zeros((SLOTS * 8, 128), F32)
    own = lane_iota((64, 128)) % 8 == lax.broadcasted_iota(jnp.int32, (64, 128), 0) // 8

    def one_slot(s, carry):
        def pick(c, carry):
            for k in range(32):
                t = c * 32 + k
                gat_s[pl.ds(t, 1), :] = u_s[pl.ds(rows_sm[s, t], 1), :]
            return carry

        lax.fori_loop(0, 8, pick, 0)
        gh, gl = split(gat_s[...])
        w = slot_weights(value_ref[s], group_ref[pl.ds(s, 1), :])
        wh, wl = split(w)
        prod = mm(jnp.concatenate([wh, wl], 0), jnp.concatenate([gh, gl], 1))
        total = prod[:64, :128] + prod[64:, :128] + prod[:64, 128:]
        total = jnp.where(own, total, 0.0)
        z = total[0:8]
        for g in range(1, 8):
            z = z + total[g * 8:(g + 1) * 8]
        z_s[pl.ds(pl.multiple_of(s * 8, 8), 8), :] = z
        return carry

    lax.fori_loop(0, count_sm[0], one_slot, 0)
    spread = exact_times_ones(z_s[...], block_ones())
    mine = lane_iota((512, 128)) % 8 == lax.broadcasted_iota(jnp.int32, (512, 128), 0) % 8
    slot_terms = jnp.sum(jnp.where(mine, spread, 0.0).reshape(SLOTS, 8, 128), 1)
    onehot = (lax.broadcasted_iota(jnp.int32, (WINDOW * 16, SLOTS), 0) == window_ref[...]).astype(F32).astype(BF16)
    a, b, c = three(slot_terms)
    partial_ref[...] = mm(onehot, a) + mm(onehot, b) + mm(onehot, c)
    out_copy.wait()


def back_kernel(
    rows_sm, count_sm,
    own_ref, p1, p2, p3, p4, m1, m2, m3, m4,
    mask_ref, strength_ref, window_ref, value_ref, group_ref, rowf_ref,
    xh_ref, xl_ref, yh_ref, yl_ref,
    field_hbm,
    out_ref, becp_ref,
    w_s, tot_s, f_s, gat_s, xb_s, ah_s, al_s, sem,
):
    in_copy = pltpu.make_async_copy(field_hbm, w_s, sem)
    in_copy.start()
    tot_s[...] = own_ref[...]
    for delta, ref in ((1, p1), (2, p2), (3, p3), (4, p4)):
        n = (WINDOW - delta) * 16
        tot_s[delta * 16:, :] = tot_s[delta * 16:, :] + ref[...]
    for delta, ref in ((1, m1), (2, m2), (3, m3), (4, m4)):
        n = (WINDOW - delta) * 16
        tot_s[:n, :] = tot_s[:n, :] + ref[...]
    becp = jnp.where(mask_ref[...] > 0.0, tot_s[...], 0.0)
    becp_ref[...] = becp[REACH * 16:(REACH + 1) * 16]
    energy = becp * strength_ref[...]
    onehot = (lax.broadcasted_iota(jnp.int32, (WINDOW * 16, SLOTS), 0) == window_ref[...]).astype(F32).astype(BF16)
    a, b, c = three(energy)
    slot_energy = mm_tn(onehot, a) + mm_tn(onehot, b) + mm_tn(onehot, c)
    mine = lane_iota((512, 128)) % 8 == lax.broadcasted_iota(jnp.int32, (512, 128), 0) % 8
    wide = jnp.broadcast_to(slot_energy[:, None, :], (SLOTS, 8, 128)).reshape(SLOTS * 8, 128)
    f_s[...] = exact_times_ones(jnp.where(mine, wide, 0.0), block_ones())
    own = lane_iota((64, 128)) % 8 == lax.broadcasted_iota(jnp.int32, (64, 128), 0) // 8
    in_copy.wait()

    def one_slot(s, carry):
        w = slot_weights(value_ref[s], group_ref[pl.ds(s, 1), :])
        wh, wl = split(w)
        f = f_s[pl.ds(pl.multiple_of(s * 8, 8), 8), :]
        diag = jnp.where(own, jnp.concatenate([f] * 8, 0), 0.0)
        dh, dl = split(diag)
        terms = mm_tn(jnp.concatenate([wh, wl, wh], 0), jnp.concatenate([dh, dh, dl], 0))
        rows = jnp.broadcast_to(rowf_ref[pl.ds(s, 1), :], (NPTS, NPTS))
        same = (rows == rows.T).astype(F32).astype(BF16)
        th, tl = split(terms)
        both = mm(same, jnp.concatenate([th, tl], 1))
        combined = both[:, :128] + both[:, 128:]

        def pick(c, carry):
            for k in range(32):
                t = c * 32 + k
                gat_s[pl.ds(t, 1), :] = w_s[pl.ds(rows_sm[s, t], 1), :]
            return carry

        lax.fori_loop(0, 8, pick, 0)
        gat_s[...] = gat_s[...] + combined

        def put(c, carry):
            for k in range(32):
                t = c * 32 + k
                w_s[pl.ds(rows_sm[s, t], 1), :] = gat_s[pl.ds(t, 1), :]
            return carry

        lax.fori_loop(0, 8, put, 0)
        return carry

    lax.fori_loop(0, count_sm[0], one_slot, 0)

    for zz in range(2):
        def along_x(pair, carry, zz=zz):
            xh, xl = xh_ref[...], xl_ref[...]
            at = pl.multiple_of((zz * 32 + pair * 2) * 256, 256)
            h0, l0 = split(w_s[pl.ds(at, 256), :])
            h1, l1 = split(w_s[pl.ds(at + 256, 256), :])
            bh, bl = jnp.concatenate([h0, h1], 1), jnp.concatenate([l0, l1], 1)
            res = mm(xh, bh) + mm(xl, bh) + mm(xh, bl)
            for k in range(2):
                cols = slice(k * 128, (k + 1) * 128)
                xb_s[pair * 2 + k] = res[:128, cols] + swap_parts(res[128:, cols], 1.0)
            return carry

        lax.fori_loop(0, 16, along_x, 0)
        for half in range(2):
            def permute(kc, carry, half=half):
                base = pl.multiple_of(kc * 16, 16)
                ins = [xb_s[half * 16 + j, pl.ds(base, 16), :] for j in range(16)]
                for i, v in enumerate(exchange_blocks(ins)):
                    vh, vl = split(v)
                    lo = ((i // 8) * 2 + half) * 128
                    ah_s[pl.ds((i % 8) * 128 + base, 16), lo:lo + 128] = vh
                    al_s[pl.ds((i % 8) * 128 + base, 16), lo:lo + 128] = vl
                return carry

            lax.fori_loop(0, 8, permute, 0)
        ah, al = ah_s[...], al_s[...]
        yh, yl = yh_ref[...], yl_ref[...]
        res = mm(ah, yh) + mm(al, yh) + mm(ah, yl)
        for b in range(BANDS):
            for o in range(2):
                out_ref[pl.ds(o * 16 + zz * 8 + b, 128, stride=32), :] = res[b * 128:(b + 1) * 128, o * 128:(o + 1) * 128]


def spectrum_kernel(recv_ref, coef_ref, kin_ref, th_ref, tl_ref, out_ref):
    th, tl = th_ref[...], tl_ref[...]
    kin = kin_ref[...]
    for b in range(BANDS):
        parts = [recv_ref[pl.ds(q * 8 + b, 128, stride=32), :] for q in range(4)]
        ah, al = split(jnp.concatenate(parts, 0))
        res = mm_tn(ah, th) + mm_tn(al, th) + mm_tn(ah, tl)
        for o in range(2):
            out_ref[o, b] = res[:, o * 128:(o + 1) * 128] + kin * coef_ref[o, b]


VM = pl.BlockSpec(memory_space=pltpu.VMEM)
SM = pl.BlockSpec(memory_space=pltpu.SMEM)
ANY = pl.BlockSpec(memory_space=pl.ANY)


def params():
    return pltpu.CompilerParams(vmem_limit_bytes=VMEM_LIMIT)


def run_columns(coef):
    return pl.pallas_call(
        columns_kernel,
        out_shape=jax.ShapeDtypeStruct((4096, 128), F32),
        in_specs=[VM] * 3, out_specs=VM, compiler_params=params(), name="columns",
    )(coef, *TABLES["fz"])


def run_grid(rows, count, recv, pot, value, group, window):
    return pl.pallas_call(
        grid_kernel,
        out_shape=(jax.ShapeDtypeStruct((ROWS, 128), F32), jax.ShapeDtypeStruct((WINDOW * 16, 128), F32)),
        in_specs=[SM, SM] + [VM] * 9,
        out_specs=(ANY, VM),
        scratch_shapes=[
            pltpu.VMEM((1024, 256), BF16), pltpu.VMEM((1024, 256), BF16),
            pltpu.VMEM((1024, 512), F32),
            pltpu.VMEM((16, 256, 256), BF16), pltpu.VMEM((16, 256, 256), BF16),
            pltpu.VMEM((ROWS, 128), F32), pltpu.VMEM((ROWS, 128), F32),
            pltpu.VMEM((NPTS, 128), F32), pltpu.VMEM((SLOTS * 8, 128), F32),
            pltpu.SemaphoreType.DMA(()),
        ],
        compiler_params=params(), name="grid",
    )(rows, count, recv, pot, value, group, window, *TABLES["fy"], *TABLES["fx"])


def run_back(rows, count, partials, mask, strength, window, value, group, rowf, field):
    return pl.pallas_call(
        back_kernel,
        out_shape=(jax.ShapeDtypeStruct((4096, 128), F32), jax.ShapeDtypeStruct((16, 128), F32)),
        in_specs=[SM, SM] + [VM] * 19 + [ANY],
        out_specs=(VM, VM),
        scratch_shapes=[
            pltpu.VMEM((ROWS, 128), F32), pltpu.VMEM((WINDOW * 16, 128), F32),
            pltpu.VMEM((SLOTS * 8, 128), F32), pltpu.VMEM((NPTS, 128), F32),
            pltpu.VMEM((32, 128, 128), F32),
            pltpu.VMEM((1024, 512), BF16), pltpu.VMEM((1024, 512), BF16),
            pltpu.SemaphoreType.DMA(()),
        ],
        compiler_params=params(), name="back",
    )(rows, count, *partials, mask, strength, window, value, group, rowf, *TABLES["bx"], *TABLES["by"], field)


def run_spectrum(recv, coef, kin):
    return pl.pallas_call(
        spectrum_kernel,
        out_shape=jax.ShapeDtypeStruct((2, BANDS, 128, 128), F32),
        in_specs=[VM] * 5, out_specs=VM, compiler_params=params(), name="spectrum",
    )(recv, coef, kin, *TABLES["bz"])


def to_all(block):
    block = block.reshape(128, 32, 128)
    block = lax.all_to_all(block, "pencil", split_axis=0, concat_axis=0, tiled=True)
    return block.reshape(4096, 128)


def from_offset(block, delta):
    n = lax.axis_size("pencil")
    return lax.ppermute(block, "pencil", [((i + delta) % n, i) for i in range(n)])


def per_device(coefficients, potential, slot_atom, slot_count, point_offset, proj_value, proj_strength, proj_count):
    device = lax.axis_index("pencil")
    n_dev = lax.axis_size("pencil")
    atom_dev = proj_strength.shape[0] // n_dev
    rows = (point_offset >> 11) * 256 + (point_offset & 255)
    group = (point_offset >> 8) & 7
    rowf = rows.astype(F32)
    window = ((slot_atom // atom_dev - device + REACH) % n_dev) * atom_dev + slot_atom % atom_dev
    window = window[None, :]
    atoms = ((device - REACH) * atom_dev + jnp.arange(WINDOW * atom_dev, dtype=jnp.int32)) % (n_dev * atom_dev)
    strength = jnp.tile(proj_strength[atoms], (1, 16))
    mask = ((jnp.arange(128, dtype=jnp.int32) % NPROJ)[None, :] < proj_count[atoms][:, None]).astype(F32)
    freq = jnp.arange(CUT, dtype=jnp.int32) - CUT // 2
    freq_x = device - CUT // 2
    kinetic = 6.0 / (CUT * CUT) * ((freq_x * freq_x + freq * freq)[:, None] + (freq * freq)[None, :]).astype(F32)

    recv = to_all(run_columns(coefficients))
    field, partial = run_grid(rows, slot_count, recv, potential, proj_value, group, window)
    partials = [partial]
    for delta in range(1, 2 * REACH + 1):
        partials.append(from_offset(partial[:(WINDOW - delta) * atom_dev], delta))
    for delta in range(1, 2 * REACH + 1):
        partials.append(from_offset(partial[delta * atom_dev:], -delta))
    send, becp = run_back(rows, slot_count, partials, mask, strength, window, proj_value, group, rowf, field)
    recv = to_all(send)
    return run_spectrum(recv, coefficients, kinetic), becp


def solution(mesh):
    in_specs = (
        P(None, None, "pencil", None), P("pencil", None, None), P("pencil"), P("pencil"),
        P("pencil", None), P("pencil", None, None), P(), P(),
    )
    out_specs = (P(None, None, "pencil", None), P("pencil", None))
    return jax.shard_map(per_device, mesh=mesh, in_specs=in_specs, out_specs=out_specs, check_vma=False)
```

```python
import jax
import jax.numpy as jnp
import ml_dtypes
import numpy as np
from jax import lax
from jax.experimental import pallas as pl
from jax.experimental.pallas import tpu as pltpu
from jax.sharding import PartitionSpec as P

GRID = 256
CUT = 128
NPROJ = 8
REACH = 2
BANDS = 8
SLOTS = 64
NPTS = 256
ROWS = 16384
WINDOW = 2 * REACH + 1
F32 = jnp.float32
BF16 = jnp.bfloat16
VMEM_LIMIT = 56 * 1024 * 1024


def halves(table):
    table = np.asarray(table, np.float64)
    high = table.astype(np.float32).astype(ml_dtypes.bfloat16)
    low = (table - high.astype(np.float64)).astype(np.float32).astype(ml_dtypes.bfloat16)
    return high, low


def make_tables():
    freq = np.arange(CUT) - CUT // 2
    turns = (freq[:, None] * np.arange(GRID)[None, :]) % GRID
    cos = np.cos(2 * np.pi * turns / GRID)
    sin = np.sin(2 * np.pi * turns / GRID)
    up = CUT ** -0.5
    down = GRID ** -0.5
    planes = np.concatenate([np.arange(0, GRID, 2), np.arange(1, GRID, 2)])
    cz, sz = cos[:, planes], sin[:, planes]
    fz = up * np.block([[cz.T, -sz.T], [sz.T, cz.T]])
    fy = up * np.block([[cos, sin], [-sin, cos]])
    fx = up * np.concatenate([cos.T, sin.T], 1)
    bx = down * np.concatenate([cos, sin], 0)
    by = down * np.block([[cos.T, -sin.T], [sin.T, cos.T]])
    bz = down * np.block([[cz.T, -sz.T], [sz.T, cz.T]])
    return {k: halves(v) for k, v in dict(fz=fz, fy=fy, fx=fx, bx=bx, by=by, bz=bz).items()}


TABLES = make_tables()


def split(value):
    high = value.astype(BF16)
    low = (value - high.astype(F32)).astype(BF16)
    return high, low


def mm(a, b):
    return lax.dot_general(a, b, (((1,), (0,)), ((), ())), preferred_element_type=F32)


def mm_nt(a, b):
    return lax.dot_general(a, b, (((1,), (1,)), ((), ())), preferred_element_type=F32)


def mm_tn(a, b):
    return lax.dot_general(a, b, (((0,), (0,)), ((), ())), preferred_element_type=F32)


def lane_iota(shape):
    return lax.broadcasted_iota(jnp.int32, shape, len(shape) - 1)


def exchange_blocks(arrays):
    rows = arrays[0].shape[0]
    block = lane_iota((rows, 128)) // 8
    rolled = [pltpu.roll(a, 8 * i, 1) if i else a for i, a in enumerate(arrays)]
    vals = [rolled[(-n) % 16] for n in range(16)]
    for bit in range(4):
        step = 1 << bit
        chosen = (block // step) % 2 == 1
        vals = [jnp.where(chosen, vals[(j - step) % 16], vals[j]) for j in range(16)]
    return [pltpu.roll(v, (128 - 8 * j) % 128, 1) if j else v for j, v in enumerate(vals)]


def swap_parts(value, first_sign):
    rolled = pltpu.roll(value, 64, 1)
    first = lane_iota(value.shape) < 64
    return jnp.where(first, first_sign * rolled, -first_sign * rolled)


def block_ones():
    row = lax.broadcasted_iota(jnp.int32, (128, 128), 0) // 8
    col = lax.broadcasted_iota(jnp.int32, (128, 128), 1) // 8
    return (row == col).astype(F32)


def three(value):
    a = value.astype(BF16)
    rest = value - a.astype(F32)
    b = rest.astype(BF16)
    c = (rest - b.astype(F32)).astype(BF16)
    return a, b, c


def exact_times_ones(value, ones):
    ones = ones.astype(BF16)
    a, b, c = three(value)
    return mm(a, ones) + mm(b, ones) + mm(c, ones)


def slot_weights(values, groups):
    return jnp.concatenate([jnp.where(groups == g, values, 0.0) for g in range(8)], 0)


def columns_kernel(coef_ref, th_ref, tl_ref, out_ref):
    th, tl = th_ref[...], tl_ref[...]
    for b in range(BANDS):
        a = jnp.concatenate([coef_ref[0, b], coef_ref[1, b]], 1)
        ah, al = split(a)
        res = mm_nt(th, ah) + mm_nt(tl, ah) + mm_nt(th, al)
        for q in range(4):
            out_ref[pl.ds(q * 8 + b, 128, stride=32), :] = res[q * 128:(q + 1) * 128]


def grid_kernel(
    rows_sm, count_sm,
    recv_ref, pot_ref, value_ref, group_ref, window_ref,
    yh_ref, yl_ref, xh_ref, xl_ref,
    field_hbm, partial_ref, c1, c2, c3, c4, d1, d2, d3, d4,
    ah_s, al_s, ys_s, inh_s, inl_s, u_s, w_s, ga_s, gb_s, z_s, sem,
):
    yh, yl = yh_ref[...], yl_ref[...]
    piece = lax.broadcasted_iota(jnp.int32, (32, 128), 0)
    pick_group = (lane_iota((32, 128)) % 8 == piece % 8).astype(F32).astype(BF16)
    for zz in range(2):
        for b in range(BANDS):
            for r in range(2):
                part = recv_ref[pl.ds(r * 16 + zz * 8 + b, 128, stride=32), :]
                h, l = split(part)
                ah_s[b * 128:(b + 1) * 128, r * 128:(r + 1) * 128] = h
                al_s[b * 128:(b + 1) * 128, r * 128:(r + 1) * 128] = l
        ah, al = ah_s[...], al_s[...]
        ys_s[...] = mm(ah, yh) + mm(al, yh) + mm(ah, yl)
        for half in range(2):
            def permute(kc, carry, half=half):
                base = pl.multiple_of(kc * 16, 16)
                ins = [
                    ys_s[pl.ds((i % 8) * 128 + base, 16), ((i // 8) * 2 + half) * 128:((i // 8) * 2 + half + 1) * 128]
                    for i in range(16)
                ]
                outs = exchange_blocks(ins)
                for j, v in enumerate(outs):
                    s = swap_parts(v, -1.0)
                    pair = half * 8 + j // 2
                    cols = slice((j % 2) * 128, (j % 2 + 1) * 128)
                    vh, vl = split(v)
                    sh, sl = split(s)
                    inh_s[pair, pl.ds(base, 16), cols] = vh
                    inl_s[pair, pl.ds(base, 16), cols] = vl
                    inh_s[pair, pl.ds(128 + base, 16), cols] = sh
                    inl_s[pair, pl.ds(128 + base, 16), cols] = sl
                return carry

            lax.fori_loop(0, 8, permute, 0)

        def along_x(pair, carry, zz=zz):
            xh, xl = xh_ref[...], xl_ref[...]
            bh, bl = inh_s[pair], inl_s[pair]
            res = mm(xh, bh) + mm(xl, bh) + mm(xh, bl)
            for k in range(2):
                yg = pair * 2 + k
                pot = pot_ref[zz, pl.ds(pl.multiple_of(yg * 8, 8), 8), :]
                pa, pb, pc = three(pot)
                pieces = jnp.concatenate([pa.astype(F32), pb.astype(F32), pc.astype(F32), jnp.zeros((8, 256), F32)], 0)
                spread = mm_tn(pieces.astype(BF16), pick_group)
                u = res[:, k * 128:(k + 1) * 128]
                at = pl.multiple_of((zz * 32 + yg) * 256, 256)
                u_s[pl.ds(at, 256), :] = u
                w_s[pl.ds(at, 256), :] = u * spread
            return carry

        lax.fori_loop(0, 16, along_x, 0)
    out_copy = pltpu.make_async_copy(w_s, field_hbm, sem)
    out_copy.start()

    z_s[...] = jnp.zeros((SLOTS * 8, 128), F32)
    own = lane_iota((64, 128)) % 8 == lax.broadcasted_iota(jnp.int32, (64, 128), 0) // 8

    count = count_sm[0]

    def pick(s, buf):
        for c in range(0, NPTS, 16):
            vals = [u_s[pl.ds(rows_sm[s * NPTS + c + k], 1), :] for k in range(16)]
            for k in range(16):
                buf[c + k:c + k + 1, :] = vals[k]

    def reduce_slot(s, buf):
        gh, gl = split(buf[...])
        w = slot_weights(value_ref[s], group_ref[pl.ds(s, 1), :])
        wh, wl = split(w)
        prod = mm(jnp.concatenate([wh, wl], 0), jnp.concatenate([gh, gl], 1))
        total = prod[:64, :128] + prod[64:, :128] + prod[:64, 128:]
        total = jnp.where(own, total, 0.0)
        z = total[0:8]
        for g in range(1, 8):
            z = z + total[g * 8:(g + 1) * 8]
        z_s[pl.ds(pl.multiple_of(s * 8, 8), 8), :] = jnp.where(s < count, z, 0.0)

    def two_slots(i, carry):
        s = i * 2
        pick(s + 1, gb_s)
        reduce_slot(s, ga_s)
        pick(jnp.minimum(s + 2, SLOTS - 1), ga_s)
        reduce_slot(s + 1, gb_s)
        return carry

    pick(0, ga_s)
    lax.fori_loop(0, (count + 1) // 2, two_slots, 0)
    spread = exact_times_ones(z_s[...], block_ones())
    mine = lane_iota((512, 128)) % 8 == lax.broadcasted_iota(jnp.int32, (512, 128), 0) % 8
    slot_terms = jnp.sum(jnp.where(mine, spread, 0.0).reshape(SLOTS, 8, 128), 1)
    onehot = (lax.broadcasted_iota(jnp.int32, (WINDOW * 16, SLOTS), 0) == window_ref[...]).astype(F32).astype(BF16)
    a, b, c = three(slot_terms)
    partial = mm(onehot, a) + mm(onehot, b) + mm(onehot, c)
    partial_ref[...] = partial
    for delta, below, above in ((1, c1, d1), (2, c2, d2), (3, c3, d3), (4, c4, d4)):
        below[...] = partial[:(WINDOW - delta) * 16]
        above[...] = partial[delta * 16:]
    out_copy.wait()


def back_kernel(
    rows_sm, count_sm,
    own_ref, p1, p2, p3, p4, m1, m2, m3, m4,
    mask_ref, strength_ref, window_ref, value_ref, group_ref, rowf_ref,
    xh_ref, xl_ref, yh_ref, yl_ref,
    field_hbm,
    out_ref, becp_ref,
    w_s, tot_s, f_s, gat_s, ta_s, tb_s, xb_s, ah_s, al_s, sem,
):
    in_copy = pltpu.make_async_copy(field_hbm, w_s, sem)
    in_copy.start()
    tot_s[...] = own_ref[...]
    for delta, ref in ((1, p1), (2, p2), (3, p3), (4, p4)):
        n = (WINDOW - delta) * 16
        tot_s[delta * 16:, :] = tot_s[delta * 16:, :] + ref[...]
    for delta, ref in ((1, m1), (2, m2), (3, m3), (4, m4)):
        n = (WINDOW - delta) * 16
        tot_s[:n, :] = tot_s[:n, :] + ref[...]
    becp = jnp.where(mask_ref[...] > 0.0, tot_s[...], 0.0)
    becp_ref[...] = becp[REACH * 16:(REACH + 1) * 16]
    energy = becp * strength_ref[...]
    onehot = (lax.broadcasted_iota(jnp.int32, (WINDOW * 16, SLOTS), 0) == window_ref[...]).astype(F32).astype(BF16)
    a, b, c = three(energy)
    slot_energy = mm_tn(onehot, a) + mm_tn(onehot, b) + mm_tn(onehot, c)
    mine = lane_iota((512, 128)) % 8 == lax.broadcasted_iota(jnp.int32, (512, 128), 0) % 8
    wide = jnp.broadcast_to(slot_energy[:, None, :], (SLOTS, 8, 128)).reshape(SLOTS * 8, 128)
    f_s[...] = exact_times_ones(jnp.where(mine, wide, 0.0), block_ones())
    own = lane_iota((64, 128)) % 8 == lax.broadcasted_iota(jnp.int32, (64, 128), 0) // 8
    count = count_sm[0]

    def terms_of(s, buf):
        w = slot_weights(value_ref[s], group_ref[pl.ds(s, 1), :])
        wh, wl = split(w)
        f = f_s[pl.ds(pl.multiple_of(s * 8, 8), 8), :]
        f = jnp.where(s < count, f, 0.0)
        diag = jnp.where(own, jnp.concatenate([f] * 8, 0), 0.0)
        dh, dl = split(diag)
        terms = mm_tn(jnp.concatenate([wh, wl, wh], 0), jnp.concatenate([dh, dh, dl], 0))
        rows = jnp.broadcast_to(rowf_ref[pl.ds(s, 1), :], (NPTS, NPTS))
        same = (rows == rows.T).astype(F32).astype(BF16)
        th, tl = split(terms)
        both = mm(same, jnp.concatenate([th, tl], 1))
        buf[...] = both[:, :128] + both[:, 128:]

    def add_slot(s, buf):
        for c in range(0, NPTS, 16):
            vals = [w_s[pl.ds(rows_sm[s * NPTS + c + k], 1), :] for k in range(16)]
            for k in range(16):
                gat_s[c + k:c + k + 1, :] = vals[k]
        gat_s[...] = gat_s[...] + buf[...]
        for c in range(0, NPTS, 16):
            vals = [gat_s[c + k:c + k + 1, :] for k in range(16)]
            for k in range(16):
                w_s[pl.ds(rows_sm[s * NPTS + c + k], 1), :] = vals[k]

    def two_slots(i, carry):
        s = i * 2
        terms_of(s + 1, tb_s)
        add_slot(s, ta_s)
        terms_of(jnp.minimum(s + 2, SLOTS - 1), ta_s)
        add_slot(s + 1, tb_s)
        return carry

    terms_of(0, ta_s)
    in_copy.wait()
    lax.fori_loop(0, (count + 1) // 2, two_slots, 0)

    for zz in range(2):
        def along_x(pair, carry, zz=zz):
            xh, xl = xh_ref[...], xl_ref[...]
            at = pl.multiple_of((zz * 32 + pair * 2) * 256, 256)
            h0, l0 = split(w_s[pl.ds(at, 256), :])
            h1, l1 = split(w_s[pl.ds(at + 256, 256), :])
            bh, bl = jnp.concatenate([h0, h1], 1), jnp.concatenate([l0, l1], 1)
            res = mm(xh, bh) + mm(xl, bh) + mm(xh, bl)
            for k in range(2):
                cols = slice(k * 128, (k + 1) * 128)
                xb_s[pair * 2 + k] = res[:128, cols] + swap_parts(res[128:, cols], 1.0)
            return carry

        lax.fori_loop(0, 16, along_x, 0)
        for half in range(2):
            def permute(kc, carry, half=half):
                base = pl.multiple_of(kc * 16, 16)
                ins = [xb_s[half * 16 + j, pl.ds(base, 16), :] for j in range(16)]
                for i, v in enumerate(exchange_blocks(ins)):
                    vh, vl = split(v)
                    lo = ((i // 8) * 2 + half) * 128
                    ah_s[pl.ds((i % 8) * 128 + base, 16), lo:lo + 128] = vh
                    al_s[pl.ds((i % 8) * 128 + base, 16), lo:lo + 128] = vl
                return carry

            lax.fori_loop(0, 8, permute, 0)
        ah, al = ah_s[...], al_s[...]
        yh, yl = yh_ref[...], yl_ref[...]
        res = mm(ah, yh) + mm(al, yh) + mm(ah, yl)
        for b in range(BANDS):
            for o in range(2):
                out_ref[pl.ds(o * 16 + zz * 8 + b, 128, stride=32), :] = res[b * 128:(b + 1) * 128, o * 128:(o + 1) * 128]


def spectrum_kernel(recv_ref, coef_ref, kin_ref, th_ref, tl_ref, out_ref):
    th, tl = th_ref[...], tl_ref[...]
    kin = kin_ref[...]
    for b in range(BANDS):
        parts = [recv_ref[pl.ds(q * 8 + b, 128, stride=32), :] for q in range(4)]
        ah, al = split(jnp.concatenate(parts, 0))
        res = mm_tn(ah, th) + mm_tn(al, th) + mm_tn(ah, tl)
        for o in range(2):
            out_ref[o, b] = res[:, o * 128:(o + 1) * 128] + kin * coef_ref[o, b]


VM = pl.BlockSpec(memory_space=pltpu.VMEM)
SM = pl.BlockSpec(memory_space=pltpu.SMEM)
ANY = pl.BlockSpec(memory_space=pl.ANY)


def params():
    return pltpu.CompilerParams(vmem_limit_bytes=VMEM_LIMIT)


def run_columns(coef):
    return pl.pallas_call(
        columns_kernel,
        out_shape=jax.ShapeDtypeStruct((4096, 128), F32),
        in_specs=[VM] * 3, out_specs=VM, compiler_params=params(), name="columns",
    )(coef, *TABLES["fz"])


def run_grid(rows, count, recv, pot, value, group, window):
    return pl.pallas_call(
        grid_kernel,
        out_shape=[jax.ShapeDtypeStruct((ROWS, 128), F32)] + [
            jax.ShapeDtypeStruct((blocks * 16, 128), F32) for blocks in (5, 4, 3, 2, 1, 4, 3, 2, 1)
        ],
        in_specs=[SM, SM] + [VM] * 9,
        out_specs=[ANY] + [VM] * 9,
        scratch_shapes=[
            pltpu.VMEM((1024, 256), BF16), pltpu.VMEM((1024, 256), BF16),
            pltpu.VMEM((1024, 512), F32),
            pltpu.VMEM((16, 256, 256), BF16), pltpu.VMEM((16, 256, 256), BF16),
            pltpu.VMEM((ROWS, 128), F32), pltpu.VMEM((ROWS, 128), F32),
            pltpu.VMEM((NPTS, 128), F32), pltpu.VMEM((NPTS, 128), F32), pltpu.VMEM((SLOTS * 8, 128), F32),
            pltpu.SemaphoreType.DMA(()),
        ],
        compiler_params=params(), name="grid",
    )(rows, count, recv, pot, value, group, window, *TABLES["fy"], *TABLES["fx"])


def run_back(rows, count, partials, mask, strength, window, value, group, rowf, field):
    return pl.pallas_call(
        back_kernel,
        out_shape=(jax.ShapeDtypeStruct((4096, 128), F32), jax.ShapeDtypeStruct((16, 128), F32)),
        in_specs=[SM, SM] + [VM] * 19 + [ANY],
        out_specs=(VM, VM),
        scratch_shapes=[
            pltpu.VMEM((ROWS, 128), F32), pltpu.VMEM((WINDOW * 16, 128), F32),
            pltpu.VMEM((SLOTS * 8, 128), F32), pltpu.VMEM((NPTS, 128), F32),
            pltpu.VMEM((NPTS, 128), F32), pltpu.VMEM((NPTS, 128), F32),
            pltpu.VMEM((32, 128, 128), F32),
            pltpu.VMEM((1024, 512), BF16), pltpu.VMEM((1024, 512), BF16),
            pltpu.SemaphoreType.DMA(()),
        ],
        compiler_params=params(), name="back",
    )(rows, count, *partials, mask, strength, window, value, group, rowf, *TABLES["bx"], *TABLES["by"], field)


def run_spectrum(recv, coef, kin):
    return pl.pallas_call(
        spectrum_kernel,
        out_shape=jax.ShapeDtypeStruct((2, BANDS, 128, 128), F32),
        in_specs=[VM] * 5, out_specs=VM, compiler_params=params(), name="spectrum",
    )(recv, coef, kin, *TABLES["bz"])


def to_all(block):
    block = block.reshape(128, 32, 128)
    block = lax.all_to_all(block, "pencil", split_axis=0, concat_axis=0, tiled=True)
    return block.reshape(4096, 128)


def from_offset(block, delta):
    n = lax.axis_size("pencil")
    return lax.ppermute(block, "pencil", [((i + delta) % n, i) for i in range(n)])


def per_device(coefficients, potential, slot_atom, slot_count, point_offset, proj_value, proj_strength, proj_count):
    device = lax.axis_index("pencil")
    n_dev = lax.axis_size("pencil")
    atom_dev = proj_strength.shape[0] // n_dev
    rows = (point_offset >> 11) * 256 + (point_offset & 255)
    group = (point_offset >> 8) & 7
    rowf = rows.astype(F32)
    rows = rows.reshape(-1)
    window = ((slot_atom // atom_dev - device + REACH) % n_dev) * atom_dev + slot_atom % atom_dev
    window = window[None, :]
    atoms = ((device - REACH) * atom_dev + jnp.arange(WINDOW * atom_dev, dtype=jnp.int32)) % (n_dev * atom_dev)
    strength = jnp.tile(proj_strength[atoms], (1, 16))
    mask = ((jnp.arange(128, dtype=jnp.int32) % NPROJ)[None, :] < proj_count[atoms][:, None]).astype(F32)
    freq = jnp.arange(CUT, dtype=jnp.int32) - CUT // 2
    freq_x = device - CUT // 2
    kinetic = 6.0 / (CUT * CUT) * ((freq_x * freq_x + freq * freq)[:, None] + (freq * freq)[None, :]).astype(F32)

    recv = to_all(run_columns(coefficients))
    field, partial, *windows = run_grid(rows, slot_count, recv, potential, proj_value, group, window)
    deltas = (1, 2, 3, 4, -1, -2, -3, -4)
    partials = [partial] + [from_offset(block, delta) for block, delta in zip(windows, deltas)]
    send, becp = run_back(rows, slot_count, partials, mask, strength, window, proj_value, group, rowf, field)
    recv = to_all(send)
    return run_spectrum(recv, coefficients, kinetic), becp


def solution(mesh):
    in_specs = (
        P(None, None, "pencil", None), P("pencil", None, None), P("pencil"), P("pencil"),
        P("pencil", None), P("pencil", None, None), P(), P(),
    )
    out_specs = (P(None, None, "pencil", None), P("pencil", None))
    return jax.shard_map(per_device, mesh=mesh, in_specs=in_specs, out_specs=out_specs, check_vma=False)
```

```python
import jax
import jax.numpy as jnp
import ml_dtypes
import numpy as np
from jax import lax
from jax.experimental import pallas as pl
from jax.experimental.pallas import tpu as pltpu
from jax.sharding import PartitionSpec as P

GRID = 256
CUT = 128
NPROJ = 8
REACH = 2
BANDS = 8
SLOTS = 64
NPTS = 256
ROWS = 16384
WINDOW = 2 * REACH + 1
F32 = jnp.float32
BF16 = jnp.bfloat16
UNROLL = 4
TO_GRID = CUT ** -1.5
TO_WAVES = GRID ** -1.5
VMEM_LIMIT = 56 * 1024 * 1024


def halves(table):
    table = np.asarray(table, np.float64)
    high = table.astype(np.float32).astype(ml_dtypes.bfloat16)
    low = (table - high.astype(np.float64)).astype(np.float32).astype(ml_dtypes.bfloat16)
    return high, low


def make_tables():
    freq = np.arange(CUT) - CUT // 2
    turns = (freq[:, None] * np.arange(GRID)[None, :]) % GRID
    cos = np.cos(2 * np.pi * turns / GRID)
    sin = np.sin(2 * np.pi * turns / GRID)
    planes = np.concatenate([np.arange(0, GRID, 2), np.arange(1, GRID, 2)])
    cz, sz = cos[:, planes], sin[:, planes]
    tables = dict(
        z=np.block([[cz.T, -sz.T], [sz.T, cz.T]]),
        y=np.block([[cos, sin], [-sin, cos]]),
        fx=np.concatenate([cos.T, sin.T], 1),
        bx=np.concatenate([cos, sin], 0),
    )
    return {name: halves(table) for name, table in tables.items()}


TABLES = make_tables()


def split(value):
    high = value.astype(BF16)
    low = (value - high.astype(F32)).astype(BF16)
    return high, low


def mm(a, b):
    return lax.dot_general(a, b, (((1,), (0,)), ((), ())), preferred_element_type=F32)


def mm_nt(a, b):
    return lax.dot_general(a, b, (((1,), (1,)), ((), ())), preferred_element_type=F32)


def mm_tn(a, b):
    return lax.dot_general(a, b, (((0,), (0,)), ((), ())), preferred_element_type=F32)


def mm_three(table_high, table_low, high, low):
    return mm(jnp.concatenate([table_high, table_low, table_high], 1), jnp.concatenate([high, high, low], 0))


def mm_three_right(high, low, table_high, table_low):
    return mm(jnp.concatenate([high, low, high], 1), jnp.concatenate([table_high, table_high, table_low], 0))


def lane_iota(shape):
    return lax.broadcasted_iota(jnp.int32, shape, len(shape) - 1)


def exchange_blocks(arrays):
    rows = arrays[0].shape[0]
    block = lane_iota((rows, 128)) // 8
    rolled = [pltpu.roll(a, 8 * i, 1) if i else a for i, a in enumerate(arrays)]
    vals = [rolled[(-n) % 16] for n in range(16)]
    for bit in range(4):
        step = 1 << bit
        chosen = (block // step) % 2 == 1
        vals = [jnp.where(chosen, vals[(j - step) % 16], vals[j]) for j in range(16)]
    return [pltpu.roll(v, (128 - 8 * j) % 128, 1) if j else v for j, v in enumerate(vals)]


def swap_parts(value, first_sign):
    sign = jnp.where(lane_iota(value.shape) < 64, first_sign, -first_sign)
    return pltpu.roll(value, 64, 1) * sign


def block_ones():
    row = lax.broadcasted_iota(jnp.int32, (128, 128), 0) // 8
    col = lax.broadcasted_iota(jnp.int32, (128, 128), 1) // 8
    return (row == col).astype(F32)


def three(value):
    a = value.astype(BF16)
    rest = value - a.astype(F32)
    b = rest.astype(BF16)
    c = (rest - b.astype(F32)).astype(BF16)
    return a, b, c


def exact_times_ones(value, ones):
    ones = ones.astype(BF16)
    a, b, c = three(value)
    return mm(a, ones) + mm(b, ones) + mm(c, ones)


def slot_weights(values, groups):
    return jnp.concatenate([jnp.where(groups == g, values, 0.0) for g in range(8)], 0)


def columns_kernel(coef_ref, th_ref, tl_ref, out_ref):
    th, tl = th_ref[...], tl_ref[...]
    for b in range(BANDS):
        a = jnp.concatenate([coef_ref[0, b], coef_ref[1, b]], 1)
        ah, al = split(a)
        res = mm_nt(jnp.concatenate([th, tl, th], 1), jnp.concatenate([ah, ah, al], 1))
        for q in range(4):
            out_ref[pl.ds(q * 8 + b, 128, stride=32), :] = TO_GRID * res[q * 128:(q + 1) * 128]


def grid_kernel(
    rows_sm, count_sm,
    recv_ref, pot_ref, value_ref, group_ref, window_ref,
    yh_ref, yl_ref, xh_ref, xl_ref,
    field_hbm, partial_ref, c1, c2, c3, c4, d1, d2, d3, d4,
    ah_s, al_s, ys_s, inha_s, inla_s, inhb_s, inlb_s, u_s, w_s, ga_s, gb_s, z_s, sem,
):
    yh, yl = yh_ref[...], yl_ref[...]
    piece = lax.broadcasted_iota(jnp.int32, (32, 128), 0)
    pick_group = (lane_iota((32, 128)) % 8 == piece % 8).astype(F32).astype(BF16)
    for zz in range(2):
        for b in range(BANDS):
            for r in range(2):
                part = recv_ref[pl.ds(r * 16 + zz * 8 + b, 128, stride=32), :]
                h, l = split(part)
                ah_s[b * 128:(b + 1) * 128, r * 128:(r + 1) * 128] = h
                al_s[b * 128:(b + 1) * 128, r * 128:(r + 1) * 128] = l
        ys_s[zz] = mm_three_right(ah_s[...], al_s[...], yh, yl)

    def permute(unit, kc):
        zz, half = unit // 2, unit % 2
        base = pl.multiple_of(kc * 16, 16)
        ins = [
            ys_s[zz, pl.ds((i % 8) * 128 + base, 16), ((i // 8) * 2 + half) * 128:((i // 8) * 2 + half + 1) * 128]
            for i in range(16)
        ]
        for j, v in enumerate(exchange_blocks(ins)):
            cols = slice((j % 2) * 128, (j % 2 + 1) * 128)
            vh, vl = split(v)
            sh, sl = split(swap_parts(v, -1.0))
            inh_s, inl_s = buffers[unit % 2]
            inh_s[j // 2, pl.ds(base, 16), cols] = vh
            inl_s[j // 2, pl.ds(base, 16), cols] = vl
            inh_s[j // 2, pl.ds(128 + base, 16), cols] = sh
            inl_s[j // 2, pl.ds(128 + base, 16), cols] = sl

    def along_x(unit, pair):
        zz, half = unit // 2, unit % 2
        inh_s, inl_s = buffers[unit % 2]
        res = mm_three(xh_ref[...], xl_ref[...], inh_s[pair], inl_s[pair])
        for k in range(2):
            yg = half * 16 + pair * 2 + k
            pot = pot_ref[zz, pl.ds(pl.multiple_of(yg * 8, 8), 8), :]
            pa, pb, pc = three(pot)
            pieces = jnp.concatenate([pa.astype(F32), pb.astype(F32), pc.astype(F32), jnp.zeros((8, 256), F32)], 0)
            spread = mm_tn(pieces.astype(BF16), pick_group)
            u = res[:, k * 128:(k + 1) * 128]
            at = pl.multiple_of((zz * 32 + yg) * 256, 256)
            u_s[pl.ds(at, 256), :] = u
            w_s[pl.ds(at, 256), :] = u * spread

    buffers = ((inha_s, inla_s), (inhb_s, inlb_s))
    for unit in range(-1, 4):
        def step(i, carry, unit=unit):
            if unit >= 0:
                along_x(unit, i)
            if unit < 3:
                permute(unit + 1, i)
            return carry

        lax.fori_loop(0, 8, step, 0, unroll=UNROLL)
    out_copy = pltpu.make_async_copy(w_s, field_hbm, sem)
    out_copy.start()

    z_s[...] = jnp.zeros((SLOTS * 8, 128), F32)
    own = lane_iota((64, 128)) % 8 == lax.broadcasted_iota(jnp.int32, (64, 128), 0) // 8

    count = count_sm[0]

    def pick(s, buf):
        for c in range(0, NPTS, 16):
            vals = [u_s[pl.ds(rows_sm[s * NPTS + c + k], 1), :] for k in range(16)]
            for k in range(16):
                buf[c + k:c + k + 1, :] = vals[k]

    def reduce_slot(s, buf):
        gh, gl = split(buf[...])
        w = slot_weights(value_ref[s], group_ref[pl.ds(s, 1), :])
        wh, wl = split(w)
        prod = mm(jnp.concatenate([wh, wl], 0), jnp.concatenate([gh, gl], 1))
        total = prod[:64, :128] + prod[64:, :128] + prod[:64, 128:]
        total = jnp.where(own, total, 0.0)
        z = total[0:8]
        for g in range(1, 8):
            z = z + total[g * 8:(g + 1) * 8]
        z_s[pl.ds(pl.multiple_of(s * 8, 8), 8), :] = jnp.where(s < count, z, 0.0)

    def two_slots(i, carry):
        s = i * 2
        pick(s + 1, gb_s)
        reduce_slot(s, ga_s)
        pick(jnp.minimum(s + 2, SLOTS - 1), ga_s)
        reduce_slot(s + 1, gb_s)
        return carry

    pick(0, ga_s)
    lax.fori_loop(0, (count + 1) // 2, two_slots, 0)
    spread = exact_times_ones(z_s[...], block_ones())
    mine = lane_iota((512, 128)) % 8 == lax.broadcasted_iota(jnp.int32, (512, 128), 0) % 8
    slot_terms = jnp.sum(jnp.where(mine, spread, 0.0).reshape(SLOTS, 8, 128), 1)
    onehot = (lax.broadcasted_iota(jnp.int32, (WINDOW * 16, SLOTS), 0) == window_ref[...]).astype(F32).astype(BF16)
    a, b, c = three(slot_terms)
    partial = mm(onehot, a) + mm(onehot, b) + mm(onehot, c)
    partial_ref[...] = partial
    for delta, below, above in ((1, c1, d1), (2, c2, d2), (3, c3, d3), (4, c4, d4)):
        below[...] = partial[:(WINDOW - delta) * 16]
        above[...] = partial[delta * 16:]
    out_copy.wait()


def back_kernel(
    rows_sm, count_sm,
    own_ref, p1, p2, p3, p4, m1, m2, m3, m4,
    mask_ref, strength_ref, window_ref, value_ref, group_ref, rowf_ref,
    xh_ref, xl_ref, yh_ref, yl_ref,
    field_hbm,
    out_ref, becp_ref,
    w_s, tot_s, f_s, gat_s, ta_s, tb_s, xa_s, xb_s, ah_s, al_s, sem,
):
    in_copy = pltpu.make_async_copy(field_hbm, w_s, sem)
    in_copy.start()
    tot_s[...] = own_ref[...]
    for delta, ref in ((1, p1), (2, p2), (3, p3), (4, p4)):
        n = (WINDOW - delta) * 16
        tot_s[delta * 16:, :] = tot_s[delta * 16:, :] + ref[...]
    for delta, ref in ((1, m1), (2, m2), (3, m3), (4, m4)):
        n = (WINDOW - delta) * 16
        tot_s[:n, :] = tot_s[:n, :] + ref[...]
    becp = jnp.where(mask_ref[...] > 0.0, tot_s[...], 0.0)
    becp_ref[...] = becp[REACH * 16:(REACH + 1) * 16]
    energy = becp * strength_ref[...]
    onehot = (lax.broadcasted_iota(jnp.int32, (WINDOW * 16, SLOTS), 0) == window_ref[...]).astype(F32).astype(BF16)
    a, b, c = three(energy)
    slot_energy = mm_tn(onehot, a) + mm_tn(onehot, b) + mm_tn(onehot, c)
    mine = lane_iota((512, 128)) % 8 == lax.broadcasted_iota(jnp.int32, (512, 128), 0) % 8
    wide = jnp.broadcast_to(slot_energy[:, None, :], (SLOTS, 8, 128)).reshape(SLOTS * 8, 128)
    f_s[...] = exact_times_ones(jnp.where(mine, wide, 0.0), block_ones())
    own = lane_iota((64, 128)) % 8 == lax.broadcasted_iota(jnp.int32, (64, 128), 0) // 8
    count = count_sm[0]

    def terms_of(s, buf):
        w = slot_weights(value_ref[s], group_ref[pl.ds(s, 1), :])
        wh, wl = split(w)
        f = f_s[pl.ds(pl.multiple_of(s * 8, 8), 8), :]
        f = jnp.where(s < count, f, 0.0)
        diag = jnp.where(own, jnp.concatenate([f] * 8, 0), 0.0)
        dh, dl = split(diag)
        terms = mm_tn(jnp.concatenate([wh, wl, wh], 0), jnp.concatenate([dh, dh, dl], 0))
        rows = jnp.broadcast_to(rowf_ref[pl.ds(s, 1), :], (NPTS, NPTS))
        same = (rows == rows.T).astype(F32).astype(BF16)
        th, tl = split(terms)
        both = mm(same, jnp.concatenate([th, tl], 1))
        buf[...] = both[:, :128] + both[:, 128:]

    def add_slot(s, buf):
        for c in range(0, NPTS, 16):
            vals = [w_s[pl.ds(rows_sm[s * NPTS + c + k], 1), :] for k in range(16)]
            for k in range(16):
                gat_s[c + k:c + k + 1, :] = vals[k]
        gat_s[...] = gat_s[...] + buf[...]
        for c in range(0, NPTS, 16):
            vals = [gat_s[c + k:c + k + 1, :] for k in range(16)]
            for k in range(16):
                w_s[pl.ds(rows_sm[s * NPTS + c + k], 1), :] = vals[k]

    def two_slots(i, carry):
        s = i * 2
        terms_of(s + 1, tb_s)
        add_slot(s, ta_s)
        terms_of(jnp.minimum(s + 2, SLOTS - 1), ta_s)
        add_slot(s + 1, tb_s)
        return carry

    terms_of(0, ta_s)
    in_copy.wait()
    lax.fori_loop(0, (count + 1) // 2, two_slots, 0)

    def along_x(unit, pair):
        zz, half = unit // 2, unit % 2
        at = pl.multiple_of((zz * 32 + half * 16 + pair * 2) * 256, 256)
        h0, l0 = split(w_s[pl.ds(at, 256), :])
        h1, l1 = split(w_s[pl.ds(at + 256, 256), :])
        bh, bl = jnp.concatenate([h0, h1], 1), jnp.concatenate([l0, l1], 1)
        res = mm_three(xh_ref[...], xl_ref[...], bh, bl)
        for k in range(2):
            cols = slice(k * 128, (k + 1) * 128)
            buffers[unit % 2][pair * 2 + k] = res[:128, cols] + swap_parts(res[128:, cols], 1.0)

    def permute(unit, kc):
        half = unit % 2
        base = pl.multiple_of(kc * 16, 16)
        ins = [buffers[unit % 2][j, pl.ds(base, 16), :] for j in range(16)]
        for i, v in enumerate(exchange_blocks(ins)):
            vh, vl = split(v)
            lo = ((i // 8) * 2 + half) * 128
            ah_s[pl.ds((i % 8) * 128 + base, 16), lo:lo + 128] = vh
            al_s[pl.ds((i % 8) * 128 + base, 16), lo:lo + 128] = vl

    buffers = (xa_s, xb_s)
    for unit in range(-1, 4):
        def step(i, carry, unit=unit):
            if unit < 3:
                along_x(unit + 1, i)
            if unit >= 0:
                permute(unit, i)
            return carry

        lax.fori_loop(0, 8, step, 0, unroll=UNROLL)
        if unit in (1, 3):
            zz = unit // 2
            yh, yl = yh_ref[...], yl_ref[...]
            ah, al = ah_s[...], al_s[...]
            res = mm_nt(jnp.concatenate([ah, al, ah], 1), jnp.concatenate([yh, yh, yl], 1))
            for b in range(BANDS):
                for o in range(2):
                    part = res[b * 128:(b + 1) * 128, o * 128:(o + 1) * 128]
                    out_ref[pl.ds(o * 16 + zz * 8 + b, 128, stride=32), :] = part


def spectrum_kernel(recv_ref, coef_ref, kin_ref, th_ref, tl_ref, out_ref):
    th, tl = th_ref[...], tl_ref[...]
    kin = kin_ref[...]
    for b in range(BANDS):
        parts = [recv_ref[pl.ds(q * 8 + b, 128, stride=32), :] for q in range(4)]
        ah, al = split(jnp.concatenate(parts, 0))
        res = mm_tn(jnp.concatenate([ah, al, ah], 0), jnp.concatenate([th, th, tl], 0))
        for o in range(2):
            out_ref[o, b] = TO_WAVES * res[:, o * 128:(o + 1) * 128] + kin * coef_ref[o, b]


VM = pl.BlockSpec(memory_space=pltpu.VMEM)
SM = pl.BlockSpec(memory_space=pltpu.SMEM)
ANY = pl.BlockSpec(memory_space=pl.ANY)
SEND = pltpu.VMEM((4096, 128), F32)


def params():
    return pltpu.CompilerParams(vmem_limit_bytes=VMEM_LIMIT)


def run_columns(coef):
    return pl.pallas_call(
        columns_kernel,
        out_shape=SEND,
        in_specs=[VM] * 3, out_specs=VM, compiler_params=params(), name="columns",
    )(coef, *TABLES["z"])


def run_grid(rows, count, recv, pot, value, group, window):
    return pl.pallas_call(
        grid_kernel,
        out_shape=[jax.ShapeDtypeStruct((ROWS, 128), F32)] + [
            pltpu.VMEM((blocks * 16, 128), F32) for blocks in (5, 4, 3, 2, 1, 4, 3, 2, 1)
        ],
        in_specs=[SM, SM] + [VM] * 9,
        out_specs=[ANY] + [VM] * 9,
        scratch_shapes=[
            pltpu.VMEM((1024, 256), BF16), pltpu.VMEM((1024, 256), BF16),
            pltpu.VMEM((2, 1024, 512), F32),
            pltpu.VMEM((8, 256, 256), BF16), pltpu.VMEM((8, 256, 256), BF16),
            pltpu.VMEM((8, 256, 256), BF16), pltpu.VMEM((8, 256, 256), BF16),
            pltpu.VMEM((ROWS, 128), F32), pltpu.VMEM((ROWS, 128), F32),
            pltpu.VMEM((NPTS, 128), F32), pltpu.VMEM((NPTS, 128), F32), pltpu.VMEM((SLOTS * 8, 128), F32),
            pltpu.SemaphoreType.DMA(()),
        ],
        compiler_params=params(), name="grid",
    )(rows, count, recv, pot, value, group, window, *TABLES["y"], *TABLES["fx"])


def run_back(rows, count, partials, mask, strength, window, value, group, rowf, field):
    return pl.pallas_call(
        back_kernel,
        out_shape=(SEND, jax.ShapeDtypeStruct((16, 128), F32)),
        in_specs=[SM, SM] + [VM] * 19 + [ANY],
        out_specs=(VM, VM),
        scratch_shapes=[
            pltpu.VMEM((ROWS, 128), F32), pltpu.VMEM((WINDOW * 16, 128), F32),
            pltpu.VMEM((SLOTS * 8, 128), F32), pltpu.VMEM((NPTS, 128), F32),
            pltpu.VMEM((NPTS, 128), F32), pltpu.VMEM((NPTS, 128), F32),
            pltpu.VMEM((16, 128, 128), F32), pltpu.VMEM((16, 128, 128), F32),
            pltpu.VMEM((1024, 512), BF16), pltpu.VMEM((1024, 512), BF16),
            pltpu.SemaphoreType.DMA(()),
        ],
        compiler_params=params(), name="back",
    )(rows, count, *partials, mask, strength, window, value, group, rowf, *TABLES["bx"], *TABLES["y"], field)


def run_spectrum(recv, coef, kin):
    return pl.pallas_call(
        spectrum_kernel,
        out_shape=jax.ShapeDtypeStruct((2, BANDS, 128, 128), F32),
        in_specs=[VM] * 5, out_specs=VM, compiler_params=params(), name="spectrum",
    )(recv, coef, kin, *TABLES["z"])


def to_all(block):
    block = block.reshape(128, 32, 128)
    block = lax.all_to_all(block, "pencil", split_axis=0, concat_axis=0, tiled=True)
    return pltpu.with_memory_space_constraint(block.reshape(4096, 128), pltpu.VMEM)


def from_offset(block, delta):
    n = lax.axis_size("pencil")
    block = lax.ppermute(block, "pencil", [((i + delta) % n, i) for i in range(n)])
    return pltpu.with_memory_space_constraint(block, pltpu.VMEM)


def per_device(coefficients, potential, slot_atom, slot_count, point_offset, proj_value, proj_strength, proj_count):
    device = lax.axis_index("pencil")
    n_dev = lax.axis_size("pencil")
    atom_dev = proj_strength.shape[0] // n_dev
    rows = (point_offset >> 11) * 256 + (point_offset & 255)
    group = (point_offset >> 8) & 7
    rowf = rows.astype(F32)
    rows = rows.reshape(-1)
    window = ((slot_atom // atom_dev - device + REACH) % n_dev) * atom_dev + slot_atom % atom_dev
    window = window[None, :]
    atoms = ((device - REACH) * atom_dev + jnp.arange(WINDOW * atom_dev, dtype=jnp.int32)) % (n_dev * atom_dev)
    strength = jnp.tile(proj_strength[atoms], (1, 16))
    mask = ((jnp.arange(128, dtype=jnp.int32) % NPROJ)[None, :] < proj_count[atoms][:, None]).astype(F32)
    freq = jnp.arange(CUT, dtype=jnp.int32) - CUT // 2
    freq_x = device - CUT // 2
    kinetic = 6.0 / (CUT * CUT) * ((freq_x * freq_x + freq * freq)[:, None] + (freq * freq)[None, :]).astype(F32)

    recv = to_all(run_columns(coefficients))
    prepared = (recv, rows, group, rowf, window, strength, mask, kinetic)
    recv, rows, group, rowf, window, strength, mask, kinetic = lax.optimization_barrier(prepared)
    field, partial, *windows = run_grid(rows, slot_count, recv, potential, proj_value, group, window)
    deltas = (1, 2, 3, 4, -1, -2, -3, -4)
    partials = [pltpu.with_memory_space_constraint(partial, pltpu.VMEM)] + [from_offset(block, delta) for block, delta in zip(windows, deltas)]
    send, becp = run_back(rows, slot_count, partials, mask, strength, window, proj_value, group, rowf, field)
    recv = to_all(send)
    return run_spectrum(recv, coefficients, kinetic), becp


def solution(mesh):
    in_specs = (
        P(None, None, "pencil", None), P("pencil", None, None), P("pencil"), P("pencil"),
        P("pencil", None), P("pencil", None, None), P(), P(),
    )
    out_specs = (P(None, None, "pencil", None), P("pencil", None))
    return jax.shard_map(per_device, mesh=mesh, in_specs=in_specs, out_specs=out_specs, check_vma=False)
```

```python
import jax
import jax.numpy as jnp
import ml_dtypes
import numpy as np
from jax import lax
from jax.experimental import pallas as pl
from jax.experimental.pallas import tpu as pltpu
from jax.sharding import PartitionSpec as P

GRID = 256
CUT = 128
NPROJ = 8
REACH = 2
BANDS = 8
SLOTS = 64
NPTS = 256
ROWS = 16384
WINDOW = 2 * REACH + 1
F32 = jnp.float32
BF16 = jnp.bfloat16
UNROLL = 4
BATCH = 16
TO_GRID = CUT ** -1.5
TO_WAVES = GRID ** -1.5


def halves(table):
    table = np.asarray(table, np.float64)
    high = table.astype(np.float32).astype(ml_dtypes.bfloat16)
    low = (table - high.astype(np.float64)).astype(np.float32).astype(ml_dtypes.bfloat16)
    return high, low


def make_tables():
    freq = np.arange(CUT) - CUT // 2
    turns = (freq[:, None] * np.arange(GRID)[None, :]) % GRID
    cos = np.cos(2 * np.pi * turns / GRID)
    sin = np.sin(2 * np.pi * turns / GRID)
    forward = np.block([[cos, sin], [-sin, cos]])
    return dict(f=halves(forward), ft=halves(forward.T))


TABLES = make_tables()


def split(value):
    high = value.astype(BF16)
    low = (value - high.astype(F32)).astype(BF16)
    return high, low


def mm(a, b):
    return lax.dot_general(a, b, (((1,), (0,)), ((), ())), preferred_element_type=F32)


def mm_nt(a, b):
    return lax.dot_general(a, b, (((1,), (1,)), ((), ())), preferred_element_type=F32)


def mm_tn(a, b):
    return lax.dot_general(a, b, (((0,), (0,)), ((), ())), preferred_element_type=F32)


def mm_three(table_high, table_low, high, low):
    return mm(jnp.concatenate([table_high, table_low, table_high], 1), jnp.concatenate([high, high, low], 0))


def mm_three_right(high, low, table_high, table_low):
    return mm(jnp.concatenate([high, low, high], 1), jnp.concatenate([table_high, table_high, table_low], 0))


def lane_iota(shape):
    return lax.broadcasted_iota(jnp.int32, shape, len(shape) - 1)


def exchange_blocks(arrays):
    rows = arrays[0].shape[0]
    block = lane_iota((rows, 128)) // 8
    rolled = [pltpu.roll(a, 8 * i, 1) if i else a for i, a in enumerate(arrays)]
    vals = [rolled[(-n) % 16] for n in range(16)]
    for bit in range(4):
        step = 1 << bit
        chosen = (block // step) % 2 == 1
        vals = [jnp.where(chosen, vals[(j - step) % 16], vals[j]) for j in range(16)]
    return [pltpu.roll(v, (128 - 8 * j) % 128, 1) if j else v for j, v in enumerate(vals)]


def swap_parts(value, first_sign):
    sign = jnp.where(lane_iota(value.shape) < 64, first_sign, -first_sign)
    return pltpu.roll(value, 64, 1) * sign


def block_ones():
    row = lax.broadcasted_iota(jnp.int32, (128, 128), 0) // 8
    col = lax.broadcasted_iota(jnp.int32, (128, 128), 1) // 8
    return (row == col).astype(F32)


def three(value):
    a = value.astype(BF16)
    rest = value - a.astype(F32)
    b = rest.astype(BF16)
    c = (rest - b.astype(F32)).astype(BF16)
    return a, b, c


def exact_times_ones(value, ones):
    ones = ones.astype(BF16)
    a, b, c = three(value)
    return mm(a, ones) + mm(b, ones) + mm(c, ones)


def slot_weights(values, groups):
    return jnp.concatenate([jnp.where(groups == g, values, 0.0) for g in range(8)], 0)


def columns_kernel(coef_ref, th_ref, tl_ref, out_ref):
    th, tl = th_ref[...], tl_ref[...]
    for b in range(BANDS):
        a = jnp.concatenate([coef_ref[0, b], coef_ref[1, b]], 1)
        ah, al = split(a)
        res = mm_nt(jnp.concatenate([th, tl, th], 1), jnp.concatenate([ah, ah, al], 1))
        for o in range(2):
            out_ref[pl.ds(o * 8 + b, 256, stride=16), :] = TO_GRID * res[o * 256:(o + 1) * 256]


def slots_kernel(count_sm, value_ref, group_ref, rowf_ref, out_ref):
    near = lax.broadcasted_iota(jnp.int32, (128, 128), 0) // BATCH == lane_iota((128, 128)) // BATCH
    low_lane = lane_iota((128, 128)) < 64

    def one_slot(s):
        w = slot_weights(value_ref[s], group_ref[pl.ds(s, 1), :])
        wh, wl = split(w)
        both = jnp.concatenate([wh, wl], 0)
        all_rows = rowf_ref[pl.ds(s, 1), :]
        for h in range(2):
            cols = slice(h * 128, (h + 1) * 128)
            rows = jnp.broadcast_to(all_rows[:, cols], (128, 128))
            same = jnp.where((rows == rows.T) & near, 1.0, 0.0).astype(BF16)
            res = mm_nt(same, both[:, cols])
            total = res + pltpu.roll(res, 64, 1)
            high = total.astype(BF16).astype(F32)
            out_ref[s, cols, :] = jnp.where(low_lane, high, total - high).astype(BF16)

    def two_slots(i, carry):
        one_slot(i * 2)
        one_slot(i * 2 + 1)
        return carry

    lax.fori_loop(0, (count_sm[0] + 1) // 2, two_slots, 0)


def grid_kernel(
    rows_sm, count_sm,
    recv_ref, pot_ref, value_ref, group_ref, window_ref,
    yh_ref, yl_ref, th_ref, tl_ref,
    w_ref, partial_ref,
    ah_s, al_s, ys_s, inha_s, inla_s, inhb_s, inlb_s, u_s, ga_s, gb_s, z_s,
):
    yh, yl = yh_ref[...], yl_ref[...]
    piece = lax.broadcasted_iota(jnp.int32, (32, 128), 0)
    pick_group = (lane_iota((32, 128)) % 8 == piece % 8).astype(F32).astype(BF16)
    for zz in range(2):
        for b in range(BANDS):
            for r in range(2):
                part = recv_ref[pl.ds(zz * 16 + r * 8 + b, 128, stride=32), :]
                h, l = split(part)
                ah_s[b * 128:(b + 1) * 128, r * 128:(r + 1) * 128] = h
                al_s[b * 128:(b + 1) * 128, r * 128:(r + 1) * 128] = l
        ys_s[zz] = mm_three_right(ah_s[...], al_s[...], yh, yl)

    def permute(unit, kc):
        zz, half = unit // 2, unit % 2
        base = pl.multiple_of(kc * 16, 16)
        ins = [
            ys_s[zz, pl.ds((i % 8) * 128 + base, 16), ((i // 8) * 2 + half) * 128:((i // 8) * 2 + half + 1) * 128]
            for i in range(16)
        ]
        for j, v in enumerate(exchange_blocks(ins)):
            cols = slice((j % 2) * 128, (j % 2 + 1) * 128)
            vh, vl = split(v)
            sh, sl = split(swap_parts(v, -1.0))
            inh_s, inl_s = buffers[unit % 2]
            inh_s[j // 2, pl.ds(base, 16), cols] = vh
            inl_s[j // 2, pl.ds(base, 16), cols] = vl
            inh_s[j // 2, pl.ds(128 + base, 16), cols] = sh
            inl_s[j // 2, pl.ds(128 + base, 16), cols] = sl

    def along_x(unit, pair):
        zz, half = unit // 2, unit % 2
        inh_s, inl_s = buffers[unit % 2]
        xh = jnp.concatenate([th_ref[:256, :128], th_ref[256:, :128]], 1)
        xl = jnp.concatenate([tl_ref[:256, :128], tl_ref[256:, :128]], 1)
        res = mm_three(xh, xl, inh_s[pair], inl_s[pair])
        for k in range(2):
            yg = half * 16 + pair * 2 + k
            pot = pot_ref[zz, pl.ds(pl.multiple_of(yg * 8, 8), 8), :]
            pa, pb, pc = three(pot)
            pieces = jnp.concatenate([pa.astype(F32), pb.astype(F32), pc.astype(F32), jnp.zeros((8, 256), F32)], 0)
            spread = mm_tn(pieces.astype(BF16), pick_group)
            u = res[:, k * 128:(k + 1) * 128]
            at = pl.multiple_of((zz * 32 + yg) * 256, 256)
            u_s[pl.ds(at, 256), :] = u
            w_ref[pl.ds(at, 256), :] = u * spread

    buffers = ((inha_s, inla_s), (inhb_s, inlb_s))
    for unit in range(-1, 4):
        def step(i, carry, unit=unit):
            if unit >= 0:
                along_x(unit, i)
            if unit < 3:
                permute(unit + 1, i)
            return carry

        lax.fori_loop(0, 8, step, 0, unroll=UNROLL)
    z_s[...] = jnp.zeros((SLOTS * 8, 128), F32)
    own = lane_iota((64, 128)) % 8 == lax.broadcasted_iota(jnp.int32, (64, 128), 0) // 8

    count = count_sm[0]

    def pick(s, buf):
        for c in range(0, NPTS, 16):
            vals = [u_s[pl.ds(rows_sm[s * NPTS + c + k], 1), :] for k in range(16)]
            for k in range(16):
                buf[c + k:c + k + 1, :] = vals[k]

    def reduce_slot(s, buf):
        gh, gl = split(buf[...])
        w = slot_weights(value_ref[s], group_ref[pl.ds(s, 1), :])
        wh, wl = split(w)
        prod = mm(jnp.concatenate([wh, wl], 0), jnp.concatenate([gh, gl], 1))
        total = prod[:64, :128] + prod[64:, :128] + prod[:64, 128:]
        total = jnp.where(own, total, 0.0)
        z = total[0:8]
        for g in range(1, 8):
            z = z + total[g * 8:(g + 1) * 8]
        z_s[pl.ds(pl.multiple_of(s * 8, 8), 8), :] = jnp.where(s < count, z, 0.0)

    def two_slots(i, carry):
        s = i * 2
        pick(s + 1, gb_s)
        reduce_slot(s, ga_s)
        pick(jnp.minimum(s + 2, SLOTS - 1), ga_s)
        reduce_slot(s + 1, gb_s)
        return carry

    pick(0, ga_s)
    lax.fori_loop(0, (count + 1) // 2, two_slots, 0)
    spread = exact_times_ones(z_s[...], block_ones())
    mine = lane_iota((512, 128)) % 8 == lax.broadcasted_iota(jnp.int32, (512, 128), 0) % 8
    slot_terms = jnp.sum(jnp.where(mine, spread, 0.0).reshape(SLOTS, 8, 128), 1)
    onehot = (lax.broadcasted_iota(jnp.int32, (WINDOW * 16, SLOTS), 0) == window_ref[...]).astype(F32).astype(BF16)
    a, b, c = three(slot_terms)
    partial_ref[...] = mm(onehot, a) + mm(onehot, b) + mm(onehot, c)


def back_kernel(
    rows_sm, count_sm,
    near_ref, after_ref, before_ref,
    mask_ref, strength_ref, window_ref, weight_ref,
    yh_ref, yl_ref,
    _,
    out_ref, becp_ref, w_s,
    tot_s, f_s, ta_s, tb_s, xa_s, xb_s, ah_s, al_s,
):
    tot_s[...] = near_ref[16:96]
    tot_s[32:] = tot_s[32:] + after_ref[...]
    tot_s[:48] = tot_s[:48] + before_ref[...]
    becp = jnp.where(mask_ref[...] > 0.0, tot_s[...], 0.0)
    becp_ref[...] = becp[REACH * 16:(REACH + 1) * 16]
    energy = becp * strength_ref[...]
    onehot = (lax.broadcasted_iota(jnp.int32, (WINDOW * 16, SLOTS), 0) == window_ref[...]).astype(F32).astype(BF16)
    a, b, c = three(energy)
    slot_energy = mm_tn(onehot, a) + mm_tn(onehot, b) + mm_tn(onehot, c)
    mine = lane_iota((512, 128)) % 8 == lax.broadcasted_iota(jnp.int32, (512, 128), 0) % 8
    wide = jnp.broadcast_to(slot_energy[:, None, :], (SLOTS, 8, 128)).reshape(SLOTS * 8, 128)
    f_s[...] = exact_times_ones(jnp.where(mine, wide, 0.0), block_ones())
    own = lane_iota((64, 128)) % 8 == lax.broadcasted_iota(jnp.int32, (64, 128), 0) // 8
    count = count_sm[0]

    def terms_of(s, buf):
        f = f_s[pl.ds(pl.multiple_of(s * 8, 8), 8), :]
        f = jnp.where(s < count, f, 0.0)
        diag = jnp.where(own, jnp.concatenate([f] * 8, 0), 0.0)
        pieces = jnp.concatenate(split(diag), 1)
        both = mm(weight_ref[s], jnp.concatenate([pieces, pieces], 0))
        buf[...] = both[:, :128] + both[:, 128:]

    def add_slot(s, buf):
        for c in range(0, NPTS, BATCH):
            at = [rows_sm[s * NPTS + c + k] for k in range(BATCH)]
            vals = [w_s[pl.ds(at[k], 1), :] + buf[c + k:c + k + 1, :] for k in range(BATCH)]
            for k in range(BATCH):
                w_s[pl.ds(at[k], 1), :] = vals[k]

    def two_slots(i, carry):
        s = i * 2
        terms_of(s + 1, tb_s)
        add_slot(s, ta_s)
        terms_of(jnp.minimum(s + 2, SLOTS - 1), ta_s)
        add_slot(s + 1, tb_s)
        return carry

    terms_of(0, ta_s)
    lax.fori_loop(0, (count + 1) // 2, two_slots, 0)

    def along_x(unit, pair):
        zz, half = unit // 2, unit % 2
        at = pl.multiple_of((zz * 32 + half * 16 + pair * 2) * 256, 256)
        h0, l0 = split(w_s[pl.ds(at, 256), :])
        h1, l1 = split(w_s[pl.ds(at + 256, 256), :])
        bh, bl = jnp.concatenate([h0, h1], 1), jnp.concatenate([l0, l1], 1)
        xh = jnp.concatenate([yh_ref[:128, :256], yh_ref[:128, 256:]], 0)
        xl = jnp.concatenate([yl_ref[:128, :256], yl_ref[:128, 256:]], 0)
        res = mm_three(xh, xl, bh, bl)
        for k in range(2):
            cols = slice(k * 128, (k + 1) * 128)
            buffers[unit % 2][pair * 2 + k] = res[:128, cols] + swap_parts(res[128:, cols], 1.0)

    def permute(unit, kc):
        half = unit % 2
        base = pl.multiple_of(kc * 16, 16)
        ins = [buffers[unit % 2][j, pl.ds(base, 16), :] for j in range(16)]
        for i, v in enumerate(exchange_blocks(ins)):
            vh, vl = split(v)
            lo = ((i // 8) * 2 + half) * 128
            ah_s[pl.ds((i % 8) * 128 + base, 16), lo:lo + 128] = vh
            al_s[pl.ds((i % 8) * 128 + base, 16), lo:lo + 128] = vl

    buffers = (xa_s, xb_s)
    for unit in range(-1, 4):
        def step(i, carry, unit=unit):
            if unit < 3:
                along_x(unit + 1, i)
            if unit >= 0:
                permute(unit, i)
            return carry

        lax.fori_loop(0, 8, step, 0, unroll=UNROLL)
        if unit in (1, 3):
            zz = unit // 2
            yh, yl = yh_ref[...], yl_ref[...]
            ah, al = ah_s[...], al_s[...]
            res = mm_nt(jnp.concatenate([ah, al, ah], 1), jnp.concatenate([yh, yh, yl], 1))
            for b in range(BANDS):
                for o in range(2):
                    part = res[b * 128:(b + 1) * 128, o * 128:(o + 1) * 128]
                    out_ref[pl.ds(zz * 16 + o * 8 + b, 128, stride=32), :] = part


def spectrum_kernel(recv_ref, coef_ref, kin_ref, th_ref, tl_ref, out_ref):
    th, tl = th_ref[...], tl_ref[...]
    kin = kin_ref[...]
    for b in range(BANDS):
        parts = [recv_ref[pl.ds(o * 8 + b, 256, stride=16), :] for o in range(2)]
        ah, al = split(jnp.concatenate(parts, 0))
        res = mm_tn(jnp.concatenate([ah, al, ah], 0), jnp.concatenate([th, th, tl], 0))
        for o in range(2):
            out_ref[o, b] = TO_WAVES * res[:, o * 128:(o + 1) * 128] + kin * coef_ref[o, b]


VM = pl.BlockSpec(memory_space=pltpu.VMEM)
SM = pl.BlockSpec(memory_space=pltpu.SMEM)
FIELD = pltpu.VMEM((ROWS, 128), F32)
SEND = pltpu.VMEM((4096, 128), F32)


def params(mebibytes):
    return pltpu.CompilerParams(vmem_limit_bytes=mebibytes * 1024 * 1024)


def run_columns(coef):
    return pl.pallas_call(
        columns_kernel,
        out_shape=jax.ShapeDtypeStruct((4096, 128), F32),
        in_specs=[VM] * 3, out_specs=VM, compiler_params=params(56), name="columns",
    )(coef, *TABLES["ft"])


def run_grid(rows, count, recv, pot, value, group, window):
    return pl.pallas_call(
        grid_kernel,
        out_shape=(FIELD, pltpu.VMEM((WINDOW * 16, 128), F32)),
        in_specs=[SM, SM] + [VM] * 9,
        out_specs=(VM, VM),
        scratch_shapes=[
            pltpu.VMEM((1024, 256), BF16), pltpu.VMEM((1024, 256), BF16),
            pltpu.VMEM((2, 1024, 512), F32),
            pltpu.VMEM((8, 256, 256), BF16), pltpu.VMEM((8, 256, 256), BF16),
            pltpu.VMEM((8, 256, 256), BF16), pltpu.VMEM((8, 256, 256), BF16),
            pltpu.VMEM((ROWS, 128), F32),
            pltpu.VMEM((NPTS, 128), F32), pltpu.VMEM((NPTS, 128), F32), pltpu.VMEM((SLOTS * 8, 128), F32),
        ],
        compiler_params=params(24), name="grid",
    )(rows, count, recv, pot, value, group, window, *TABLES["f"], *TABLES["ft"])


def run_slots(count, value, group, rowf):
    return pl.pallas_call(
        slots_kernel,
        out_shape=pltpu.VMEM((SLOTS, NPTS, 128), BF16),
        in_specs=[SM] + [VM] * 3, out_specs=VM, compiler_params=params(16), name="slots",
        cost_estimate=pl.CostEstimate(flops=10 ** 10, transcendentals=0, bytes_accessed=5 * 10 ** 6),
    )(count, value, group, rowf)


def run_back(rows, count, partials, mask, strength, window, weights, field):
    return pl.pallas_call(
        back_kernel,
        out_shape=(SEND, jax.ShapeDtypeStruct((16, 128), F32), FIELD),
        in_specs=[SM, SM] + [VM] * 10,
        out_specs=(VM, VM, VM),
        input_output_aliases={11: 2},
        scratch_shapes=[
            pltpu.VMEM((WINDOW * 16, 128), F32),
            pltpu.VMEM((SLOTS * 8, 128), F32),
            pltpu.VMEM((NPTS, 128), F32), pltpu.VMEM((NPTS, 128), F32),
            pltpu.VMEM((16, 128, 128), F32), pltpu.VMEM((16, 128, 128), F32),
            pltpu.VMEM((1024, 512), BF16), pltpu.VMEM((1024, 512), BF16),
        ],
        compiler_params=params(14), name="back",
    )(rows, count, *partials, mask, strength, window, weights, *TABLES["f"], field)


def run_spectrum(recv, coef, kin):
    return pl.pallas_call(
        spectrum_kernel,
        out_shape=jax.ShapeDtypeStruct((2, BANDS, 128, 128), F32),
        in_specs=[VM] * 5, out_specs=VM, compiler_params=params(16), name="spectrum",
    )(recv, coef, kin, *TABLES["ft"])


def to_all(block):
    block = block.reshape(128, 32, 128)
    block = lax.all_to_all(block, "pencil", split_axis=0, concat_axis=0, tiled=True)
    return pltpu.with_memory_space_constraint(block.reshape(4096, 128), pltpu.VMEM)


def from_offset(block, delta):
    n = lax.axis_size("pencil")
    return lax.ppermute(block, "pencil", [((i + delta) % n, i) for i in range(n)])


def per_device(coefficients, potential, slot_atom, slot_count, point_offset, proj_value, proj_strength, proj_count):
    device = lax.axis_index("pencil")
    n_dev = lax.axis_size("pencil")
    atom_dev = proj_strength.shape[0] // n_dev
    rows = (point_offset >> 11) * 256 + (point_offset & 255)
    group = (point_offset >> 8) & 7
    rowf = rows.astype(F32)
    rows = rows.reshape(-1)
    window = ((slot_atom // atom_dev - device + REACH) % n_dev) * atom_dev + slot_atom % atom_dev
    window = window[None, :]
    atoms = ((device - REACH) * atom_dev + jnp.arange(WINDOW * atom_dev, dtype=jnp.int32)) % (n_dev * atom_dev)
    strength = jnp.tile(proj_strength[atoms], (1, 16))
    mask = ((jnp.arange(128, dtype=jnp.int32) % NPROJ)[None, :] < proj_count[atoms][:, None]).astype(F32)
    freq = jnp.arange(CUT, dtype=jnp.int32) - CUT // 2
    freq_x = device - CUT // 2
    kinetic = 6.0 / (CUT * CUT) * ((freq_x * freq_x + freq * freq)[:, None] + (freq * freq)[None, :]).astype(F32)

    recv = to_all(run_columns(coefficients))
    weights = pltpu.with_memory_space_constraint(run_slots(slot_count, proj_value, group, rowf), pltpu.VMEM)
    prepared = (recv, rows, group, weights, window, strength, mask, kinetic)
    recv, rows, group, weights, window, strength, mask, kinetic = lax.optimization_barrier(prepared)
    field, partial = run_grid(rows, slot_count, recv, potential, proj_value, group, window)
    wide = jnp.pad(partial, ((16, 16), (0, 0)))
    wide = wide + jnp.pad(from_offset(partial, 1), ((32, 0), (0, 0))) + jnp.pad(from_offset(partial, -1), ((0, 32), (0, 0)))
    partials = (wide, from_offset(wide[:48], 3), from_offset(wide[64:], -3))
    partials = [pltpu.with_memory_space_constraint(block, pltpu.VMEM) for block in partials]
    field = pltpu.with_memory_space_constraint(field, pltpu.VMEM)
    send, becp, _ = run_back(rows, slot_count, partials, mask, strength, window, weights, field)
    recv = to_all(send)
    return run_spectrum(recv, coefficients, kinetic), becp


def solution(mesh):
    in_specs = (
        P(None, None, "pencil", None), P("pencil", None, None), P("pencil"), P("pencil"),
        P("pencil", None), P("pencil", None, None), P(), P(),
    )
    out_specs = (P(None, None, "pencil", None), P("pencil", None))
    return jax.shard_map(per_device, mesh=mesh, in_specs=in_specs, out_specs=out_specs, check_vma=False)
```

```python
import jax
import jax.numpy as jnp
import ml_dtypes
import numpy as np
from jax import lax
from jax.experimental import pallas as pl
from jax.experimental.pallas import tpu as pltpu
from jax.sharding import PartitionSpec as P

GRID = 256
CUT = 128
NPROJ = 8
REACH = 2
BANDS = 8
SLOTS = 64
NPTS = 256
ROWS = 16384
WINDOW = 2 * REACH + 1
F32 = jnp.float32
BF16 = jnp.bfloat16
UNROLL = 4
BATCH = 16
CHUNK = 8
TO_GRID = CUT ** -1.5
TO_WAVES = GRID ** -1.5


def halves(table):
    table = np.asarray(table, np.float64)
    high = table.astype(np.float32).astype(ml_dtypes.bfloat16)
    low = (table - high.astype(np.float64)).astype(np.float32).astype(ml_dtypes.bfloat16)
    return high, low


def make_tables():
    freq = np.arange(CUT) - CUT // 2
    turns = (freq[:, None] * np.arange(GRID)[None, :]) % GRID
    cos = np.cos(2 * np.pi * turns / GRID)
    sin = np.sin(2 * np.pi * turns / GRID)
    forward = np.block([[cos, sin], [-sin, cos]])
    return dict(f=halves(forward), ft=halves(forward.T))


TABLES = make_tables()


def split(value):
    high = value.astype(BF16)
    low = (value - high.astype(F32)).astype(BF16)
    return high, low


def mm(a, b):
    return lax.dot_general(a, b, (((1,), (0,)), ((), ())), preferred_element_type=F32)


def mm_nt(a, b):
    return lax.dot_general(a, b, (((1,), (1,)), ((), ())), preferred_element_type=F32)


def mm_tn(a, b):
    return lax.dot_general(a, b, (((0,), (0,)), ((), ())), preferred_element_type=F32)


def mm_three(table_high, table_low, high, low):
    return mm(jnp.concatenate([table_high, table_low, table_high], 1), jnp.concatenate([high, high, low], 0))


def mm_three_right(high, low, table_high, table_low):
    return mm(jnp.concatenate([high, low, high], 1), jnp.concatenate([table_high, table_high, table_low], 0))


def lane_iota(shape):
    return lax.broadcasted_iota(jnp.int32, shape, len(shape) - 1)


def exchange_blocks(arrays):
    rows = arrays[0].shape[0]
    block = lane_iota((rows, 128)) // 8
    rolled = [pltpu.roll(a, 8 * i, 1) if i else a for i, a in enumerate(arrays)]
    vals = [rolled[(-n) % 16] for n in range(16)]
    for bit in range(4):
        step = 1 << bit
        chosen = (block // step) % 2 == 1
        vals = [jnp.where(chosen, vals[(j - step) % 16], vals[j]) for j in range(16)]
    return [pltpu.roll(v, (128 - 8 * j) % 128, 1) if j else v for j, v in enumerate(vals)]


def swap_parts(value, first_sign):
    sign = jnp.where(lane_iota(value.shape) < 64, first_sign, -first_sign)
    return pltpu.roll(value, 64, 1) * sign


def block_ones():
    row = lax.broadcasted_iota(jnp.int32, (128, 128), 0) // 8
    col = lax.broadcasted_iota(jnp.int32, (128, 128), 1) // 8
    return (row == col).astype(F32)


def three(value):
    a = value.astype(BF16)
    rest = value - a.astype(F32)
    b = rest.astype(BF16)
    c = (rest - b.astype(F32)).astype(BF16)
    return a, b, c


def exact_times_ones(value, ones):
    ones = ones.astype(BF16)
    a, b, c = three(value)
    return mm(a, ones) + mm(b, ones) + mm(c, ones)


def slot_weights(values, groups):
    return jnp.concatenate([jnp.where(groups == g, values, 0.0) for g in range(8)], 0)


def columns_kernel(coef_ref, th_ref, tl_ref, out_ref):
    th, tl = th_ref[...], tl_ref[...]
    for b in range(BANDS):
        a = jnp.concatenate([coef_ref[0, b], coef_ref[1, b]], 1)
        ah, al = split(a)
        res = mm_nt(jnp.concatenate([th, tl, th], 1), jnp.concatenate([ah, ah, al], 1))
        for o in range(2):
            out_ref[pl.ds(o * 8 + b, 256, stride=16), :] = TO_GRID * res[o * 256:(o + 1) * 256]


def slots_kernel(count_sm, value_ref, group_ref, rowf_ref, out_ref):
    near = lax.broadcasted_iota(jnp.int32, (128, 128), 0) // BATCH == lane_iota((128, 128)) // BATCH
    low_lane = lane_iota((128, 128)) < 64

    def one_slot(s):
        w = slot_weights(value_ref[s], group_ref[pl.ds(s, 1), :])
        wh, wl = split(w)
        both = jnp.concatenate([wh, wl], 0)
        all_rows = rowf_ref[pl.ds(s, 1), :]
        for h in range(2):
            cols = slice(h * 128, (h + 1) * 128)
            rows = jnp.broadcast_to(all_rows[:, cols], (128, 128))
            same = jnp.where((rows == rows.T) & near, 1.0, 0.0).astype(BF16)
            res = mm_nt(same, both[:, cols])
            total = res + pltpu.roll(res, 64, 1)
            high = total.astype(BF16).astype(F32)
            out_ref[s, cols, :] = jnp.where(low_lane, high, total - high).astype(BF16)

    def two_slots(i, carry):
        one_slot(i * 2)
        one_slot(i * 2 + 1)
        return carry

    lax.fori_loop(0, (count_sm[0] + 3) // 4 * 2, two_slots, 0)


def grid_kernel(
    rows_sm, count_sm,
    pot_hbm, value_hbm, recv_ref, group_ref, window_ref,
    yh_ref, yl_ref, th_ref, tl_ref,
    field_hbm, partial_ref,
    ah_s, al_s, ys_s, inha_s, inla_s, inhb_s, inlb_s, u_s, w_s, ga_s, gb_s, z_s, pot_ref, value_ref, sem, pot_sem, value_sem,
):
    pot_copy = pltpu.make_async_copy(pot_hbm, pot_ref, pot_sem)
    pot_copy.start()
    value_copy = pltpu.make_async_copy(value_hbm, value_ref, value_sem)
    value_copy.start()
    yh, yl = yh_ref[...], yl_ref[...]
    piece = lax.broadcasted_iota(jnp.int32, (32, 128), 0)
    pick_group = (lane_iota((32, 128)) % 8 == piece % 8).astype(F32).astype(BF16)
    for zz in range(2):
        for b in range(BANDS):
            for r in range(2):
                part = recv_ref[pl.ds(zz * 16 + r * 8 + b, 128, stride=32), :]
                h, l = split(part)
                ah_s[b * 128:(b + 1) * 128, r * 128:(r + 1) * 128] = h
                al_s[b * 128:(b + 1) * 128, r * 128:(r + 1) * 128] = l
        ys_s[zz] = mm_three_right(ah_s[...], al_s[...], yh, yl)

    def permute(unit, kc):
        zz, half = unit // 2, unit % 2
        base = pl.multiple_of(kc * 16, 16)
        ins = [
            ys_s[zz, pl.ds((i % 8) * 128 + base, 16), ((i // 8) * 2 + half) * 128:((i // 8) * 2 + half + 1) * 128]
            for i in range(16)
        ]
        for j, v in enumerate(exchange_blocks(ins)):
            cols = slice((j % 2) * 128, (j % 2 + 1) * 128)
            vh, vl = split(v)
            sh, sl = split(swap_parts(v, -1.0))
            inh_s, inl_s = buffers[unit % 2]
            inh_s[j // 2, pl.ds(base, 16), cols] = vh
            inl_s[j // 2, pl.ds(base, 16), cols] = vl
            inh_s[j // 2, pl.ds(128 + base, 16), cols] = sh
            inl_s[j // 2, pl.ds(128 + base, 16), cols] = sl

    def along_x(unit, pair):
        zz, half = unit // 2, unit % 2
        inh_s, inl_s = buffers[unit % 2]
        xh = jnp.concatenate([th_ref[:256, :128], th_ref[256:, :128]], 1)
        xl = jnp.concatenate([tl_ref[:256, :128], tl_ref[256:, :128]], 1)
        res = mm_three(xh, xl, inh_s[pair], inl_s[pair])
        for k in range(2):
            yg = half * 16 + pair * 2 + k
            pot = pot_ref[zz, pl.ds(pl.multiple_of(yg * 8, 8), 8), :]
            pa, pb, pc = three(pot)
            pieces = jnp.concatenate([pa.astype(F32), pb.astype(F32), pc.astype(F32), jnp.zeros((8, 256), F32)], 0)
            spread = mm_tn(pieces.astype(BF16), pick_group)
            u = res[:, k * 128:(k + 1) * 128]
            at = pl.multiple_of((zz * 32 + yg) * 256, 256)
            u_s[pl.ds(at, 256), :] = u
            w_s[pl.ds(at, 256), :] = u * spread

    buffers = ((inha_s, inla_s), (inhb_s, inlb_s))
    for unit in range(-1, 4):
        if unit == 0:
            pot_copy.wait()

        def step(i, carry, unit=unit):
            if unit >= 0:
                along_x(unit, i)
            if unit < 3:
                permute(unit + 1, i)
            return carry

        lax.fori_loop(0, 8, step, 0, unroll=UNROLL)
    out_copy = pltpu.make_async_copy(w_s, field_hbm, sem)
    out_copy.start()
    z_s[...] = jnp.zeros((SLOTS * 8, 128), F32)
    own = lane_iota((64, 128)) % 8 == lax.broadcasted_iota(jnp.int32, (64, 128), 0) // 8

    count = count_sm[0]

    def pick(s, buf):
        for c in range(0, NPTS, 16):
            vals = [u_s[pl.ds(rows_sm[s * NPTS + c + k], 1), :] for k in range(16)]
            for k in range(16):
                buf[c + k:c + k + 1, :] = vals[k]

    def reduce_slot(s, buf):
        gh, gl = split(buf[...])
        w = slot_weights(value_ref[s], group_ref[pl.ds(s, 1), :])
        wh, wl = split(w)
        prod = mm(jnp.concatenate([wh, wl], 0), jnp.concatenate([gh, gl], 1))
        total = prod[:64, :128] + prod[64:, :128] + prod[:64, 128:]
        total = jnp.where(own, total, 0.0)
        z = total[0:8]
        for g in range(1, 8):
            z = z + total[g * 8:(g + 1) * 8]
        z_s[pl.ds(pl.multiple_of(s * 8, 8), 8), :] = jnp.where(s < count, z, 0.0)

    def two_slots(i, carry):
        s = i * 2
        pick(s + 1, gb_s)
        reduce_slot(s, ga_s)
        pick(jnp.minimum(s + 2, SLOTS - 1), ga_s)
        reduce_slot(s + 1, gb_s)
        return carry

    value_copy.wait()
    pick(0, ga_s)
    lax.fori_loop(0, (count + 1) // 2, two_slots, 0)
    spread = exact_times_ones(z_s[...], block_ones())
    mine = lane_iota((512, 128)) % 8 == lax.broadcasted_iota(jnp.int32, (512, 128), 0) % 8
    slot_terms = jnp.sum(jnp.where(mine, spread, 0.0).reshape(SLOTS, 8, 128), 1)
    onehot = (lax.broadcasted_iota(jnp.int32, (WINDOW * 16, SLOTS), 0) == window_ref[...]).astype(F32).astype(BF16)
    a, b, c = three(slot_terms)
    partial_ref[...] = mm(onehot, a) + mm(onehot, b) + mm(onehot, c)
    out_copy.wait()


def back_kernel(
    rows_sm, count_sm,
    near_ref, after_ref, before_ref,
    mask_ref, strength_ref, window_ref,
    yh_ref, yl_ref,
    weight_hbm, field_hbm,
    out_ref, becp_ref,
    w_s, weight_ref, tot_s, f_s, ta_s, tb_s, tc_s, td_s, xa_s, xb_s, ah_s, al_s, sem, chunk_sem,
):
    def chunk_copy(c):
        part = pl.ds(c * CHUNK, CHUNK)
        return pltpu.make_async_copy(weight_hbm.at[part], weight_ref.at[part], chunk_sem.at[c])

    chunk_copy(0).start()
    field_copy = pltpu.make_async_copy(field_hbm, w_s, sem)
    field_copy.start()
    for c in range(1, SLOTS // CHUNK):
        chunk_copy(c).start()

    tot_s[...] = near_ref[16:96]
    tot_s[32:] = tot_s[32:] + after_ref[...]
    tot_s[:48] = tot_s[:48] + before_ref[...]
    becp = jnp.where(mask_ref[...] > 0.0, tot_s[...], 0.0)
    becp_ref[...] = becp[REACH * 16:(REACH + 1) * 16]
    energy = becp * strength_ref[...]
    onehot = (lax.broadcasted_iota(jnp.int32, (WINDOW * 16, SLOTS), 0) == window_ref[...]).astype(F32).astype(BF16)
    a, b, c = three(energy)
    slot_energy = mm_tn(onehot, a) + mm_tn(onehot, b) + mm_tn(onehot, c)
    mine = lane_iota((512, 128)) % 8 == lax.broadcasted_iota(jnp.int32, (512, 128), 0) % 8
    wide = jnp.broadcast_to(slot_energy[:, None, :], (SLOTS, 8, 128)).reshape(SLOTS * 8, 128)
    f_s[...] = exact_times_ones(jnp.where(mine, wide, 0.0), block_ones())
    own = lane_iota((64, 128)) % 8 == lax.broadcasted_iota(jnp.int32, (64, 128), 0) // 8
    count = count_sm[0]

    def terms_of(s, buf):
        f = f_s[pl.ds(pl.multiple_of(s * 8, 8), 8), :]
        f = jnp.where(s < count, f, 0.0)
        diag = jnp.where(own, jnp.concatenate([f] * 8, 0), 0.0)
        pieces = jnp.concatenate(split(diag), 1)
        both = mm(weight_ref[s], jnp.concatenate([pieces, pieces], 0))
        buf[...] = both[:, :128] + both[:, 128:]

    def add_two(s, first, second):
        for buf, slot in ((first, s), (second, s + 1)):
            for c in range(0, NPTS, BATCH):
                at = [rows_sm[slot * NPTS + c + k] for k in range(BATCH)]
                vals = [w_s[pl.ds(at[k], 1), :] + buf[c + k:c + k + 1, :] for k in range(BATCH)]
                for k in range(BATCH):
                    w_s[pl.ds(at[k], 1), :] = vals[k]

    def four_slots(i, carry):
        s = i * 4
        later = jnp.minimum(s + 4, SLOTS - 2)

        @pl.when((lax.rem(i, 2) == 1) & (s + 4 < SLOTS))
        def _():
            chunk_copy((s + 4) // CHUNK).wait()

        terms_of(s + 2, tc_s)
        terms_of(s + 3, td_s)
        add_two(s, ta_s, tb_s)
        terms_of(later, ta_s)
        terms_of(later + 1, tb_s)
        add_two(s + 2, tc_s, td_s)
        return carry

    fours = (count + 3) // 4
    chunk_copy(0).wait()
    terms_of(0, ta_s)
    terms_of(1, tb_s)
    field_copy.wait()
    lax.fori_loop(0, fours, four_slots, 0)

    def drain(c, carry):
        chunk_copy(c).wait()
        return carry

    lax.fori_loop(jnp.minimum(fours // 2, SLOTS // CHUNK - 1) + 1, SLOTS // CHUNK, drain, 0)

    def along_x(unit, pair):
        zz, half = unit // 2, unit % 2
        at = pl.multiple_of((zz * 32 + half * 16 + pair * 2) * 256, 256)
        h0, l0 = split(w_s[pl.ds(at, 256), :])
        h1, l1 = split(w_s[pl.ds(at + 256, 256), :])
        bh, bl = jnp.concatenate([h0, h1], 1), jnp.concatenate([l0, l1], 1)
        xh = jnp.concatenate([yh_ref[:128, :256], yh_ref[:128, 256:]], 0)
        xl = jnp.concatenate([yl_ref[:128, :256], yl_ref[:128, 256:]], 0)
        res = mm_three(xh, xl, bh, bl)
        for k in range(2):
            cols = slice(k * 128, (k + 1) * 128)
            buffers[unit % 2][pair * 2 + k] = res[:128, cols] + swap_parts(res[128:, cols], 1.0)

    def permute(unit, kc):
        half = unit % 2
        base = pl.multiple_of(kc * 16, 16)
        ins = [buffers[unit % 2][j, pl.ds(base, 16), :] for j in range(16)]
        for i, v in enumerate(exchange_blocks(ins)):
            vh, vl = split(v)
            lo = ((i // 8) * 2 + half) * 128
            ah_s[pl.ds((i % 8) * 128 + base, 16), lo:lo + 128] = vh
            al_s[pl.ds((i % 8) * 128 + base, 16), lo:lo + 128] = vl

    buffers = (xa_s, xb_s)
    for unit in range(-1, 4):
        def step(i, carry, unit=unit):
            if unit < 3:
                along_x(unit + 1, i)
            if unit >= 0:
                permute(unit, i)
            return carry

        lax.fori_loop(0, 8, step, 0, unroll=UNROLL)
        if unit in (1, 3):
            zz = unit // 2
            yh, yl = yh_ref[...], yl_ref[...]
            ah, al = ah_s[...], al_s[...]
            res = mm_nt(jnp.concatenate([ah, al, ah], 1), jnp.concatenate([yh, yh, yl], 1))
            for b in range(BANDS):
                for o in range(2):
                    part = res[b * 128:(b + 1) * 128, o * 128:(o + 1) * 128]
                    out_ref[pl.ds(zz * 16 + o * 8 + b, 128, stride=32), :] = part


def spectrum_kernel(recv_ref, coef_ref, kin_ref, th_ref, tl_ref, out_ref):
    th, tl = th_ref[...], tl_ref[...]
    kin = kin_ref[...]
    for b in range(BANDS):
        parts = [recv_ref[pl.ds(o * 8 + b, 256, stride=16), :] for o in range(2)]
        ah, al = split(jnp.concatenate(parts, 0))
        res = mm_tn(jnp.concatenate([ah, al, ah], 0), jnp.concatenate([th, th, tl], 0))
        for o in range(2):
            out_ref[o, b] = TO_WAVES * res[:, o * 128:(o + 1) * 128] + kin * coef_ref[o, b]


VM = pl.BlockSpec(memory_space=pltpu.VMEM)
HBM = pl.BlockSpec(memory_space=pltpu.HBM)
SM = pl.BlockSpec(memory_space=pltpu.SMEM)
SEND = pltpu.VMEM((4096, 128), F32)


def params(mebibytes):
    return pltpu.CompilerParams(vmem_limit_bytes=mebibytes * 1024 * 1024)


def run_columns(coef):
    return pl.pallas_call(
        columns_kernel,
        out_shape=jax.ShapeDtypeStruct((4096, 128), F32),
        in_specs=[VM] * 3, out_specs=VM, compiler_params=params(56), name="columns",
    )(coef, *TABLES["ft"])


def run_grid(rows, count, recv, pot, value, group, window):
    return pl.pallas_call(
        grid_kernel,
        out_shape=(jax.ShapeDtypeStruct((ROWS, 128), F32), pltpu.VMEM((WINDOW * 16, 128), F32)),
        in_specs=[SM, SM, HBM, HBM] + [VM] * 7,
        out_specs=(HBM, VM),
        scratch_shapes=[
            pltpu.VMEM((1024, 256), BF16), pltpu.VMEM((1024, 256), BF16),
            pltpu.VMEM((2, 1024, 512), F32),
            pltpu.VMEM((8, 256, 256), BF16), pltpu.VMEM((8, 256, 256), BF16),
            pltpu.VMEM((8, 256, 256), BF16), pltpu.VMEM((8, 256, 256), BF16),
            pltpu.VMEM((ROWS, 128), F32), pltpu.VMEM((ROWS, 128), F32),
            pltpu.VMEM((NPTS, 128), F32), pltpu.VMEM((NPTS, 128), F32), pltpu.VMEM((SLOTS * 8, 128), F32),
            pltpu.VMEM((2, GRID, GRID), F32), pltpu.VMEM((SLOTS, NPROJ, NPTS), F32),
            pltpu.SemaphoreType.DMA(()), pltpu.SemaphoreType.DMA(()), pltpu.SemaphoreType.DMA(()),
        ],
        compiler_params=params(34), name="grid",
    )(rows, count, pot, value, recv, group, window, *TABLES["f"], *TABLES["ft"])


def run_slots(count, value, group, rowf):
    return pl.pallas_call(
        slots_kernel,
        out_shape=pltpu.HBM((SLOTS, NPTS, 128), BF16),
        in_specs=[SM] + [VM] * 3, out_specs=VM, compiler_params=params(16), name="slots",
        cost_estimate=pl.CostEstimate(flops=10 ** 10, transcendentals=0, bytes_accessed=5 * 10 ** 6),
    )(count, value, group, rowf)


def run_back(rows, count, partials, mask, strength, window, weights, field):
    return pl.pallas_call(
        back_kernel,
        out_shape=(SEND, jax.ShapeDtypeStruct((16, 128), F32)),
        in_specs=[SM, SM] + [VM] * 8 + [HBM, HBM],
        out_specs=(VM, VM),
        scratch_shapes=[
            pltpu.VMEM((ROWS, 128), F32), pltpu.VMEM((SLOTS, NPTS, 128), BF16),
            pltpu.VMEM((WINDOW * 16, 128), F32),
            pltpu.VMEM((SLOTS * 8, 128), F32),
            pltpu.VMEM((NPTS, 128), F32), pltpu.VMEM((NPTS, 128), F32),
            pltpu.VMEM((NPTS, 128), F32), pltpu.VMEM((NPTS, 128), F32),
            pltpu.VMEM((16, 128, 128), F32), pltpu.VMEM((16, 128, 128), F32),
            pltpu.VMEM((1024, 512), BF16), pltpu.VMEM((1024, 512), BF16),
            pltpu.SemaphoreType.DMA(()), pltpu.SemaphoreType.DMA((SLOTS // CHUNK,)),
        ],
        compiler_params=params(28), name="back",
    )(rows, count, *partials, mask, strength, window, *TABLES["f"], weights, field)


def run_spectrum(recv, coef, kin):
    return pl.pallas_call(
        spectrum_kernel,
        out_shape=jax.ShapeDtypeStruct((2, BANDS, 128, 128), F32),
        in_specs=[VM] * 5, out_specs=VM, compiler_params=params(16), name="spectrum",
    )(recv, coef, kin, *TABLES["ft"])


def to_all(block):
    block = block.reshape(128, 32, 128)
    block = lax.all_to_all(block, "pencil", split_axis=0, concat_axis=0, tiled=True)
    return pltpu.with_memory_space_constraint(block.reshape(4096, 128), pltpu.VMEM)


def from_offset(block, delta):
    n = lax.axis_size("pencil")
    return lax.ppermute(block, "pencil", [((i + delta) % n, i) for i in range(n)])


def per_device(coefficients, potential, slot_atom, slot_count, point_offset, proj_value, proj_strength, proj_count):
    device = lax.axis_index("pencil")
    n_dev = lax.axis_size("pencil")
    atom_dev = proj_strength.shape[0] // n_dev
    rows = (point_offset >> 11) * 256 + (point_offset & 255)
    group = (point_offset >> 8) & 7
    rowf = rows.astype(F32)
    rows = rows.reshape(-1)
    window = ((slot_atom // atom_dev - device + REACH) % n_dev) * atom_dev + slot_atom % atom_dev
    window = window[None, :]
    atoms = ((device - REACH) * atom_dev + jnp.arange(WINDOW * atom_dev, dtype=jnp.int32)) % (n_dev * atom_dev)
    strength = jnp.tile(proj_strength[atoms], (1, 16))
    mask = ((jnp.arange(128, dtype=jnp.int32) % NPROJ)[None, :] < proj_count[atoms][:, None]).astype(F32)
    freq = jnp.arange(CUT, dtype=jnp.int32) - CUT // 2
    freq_x = device - CUT // 2
    kinetic = 6.0 / (CUT * CUT) * ((freq_x * freq_x + freq * freq)[:, None] + (freq * freq)[None, :]).astype(F32)

    recv = to_all(run_columns(coefficients))
    weights = run_slots(slot_count, proj_value, group, rowf)
    prepared = (recv, rows, group, weights, window, strength, mask, kinetic)
    recv, rows, group, weights, window, strength, mask, kinetic = lax.optimization_barrier(prepared)
    field, partial = run_grid(rows, slot_count, recv, potential, proj_value, group, window)
    wide = jnp.pad(partial, ((16, 16), (0, 0)))
    wide = wide + jnp.pad(from_offset(partial, 1), ((32, 0), (0, 0))) + jnp.pad(from_offset(partial, -1), ((0, 32), (0, 0)))
    partials = (wide, from_offset(wide[:48], 3), from_offset(wide[64:], -3))
    partials = [pltpu.with_memory_space_constraint(block, pltpu.VMEM) for block in partials]
    field = pltpu.with_memory_space_constraint(field, pltpu.HBM)
    weights = pltpu.with_memory_space_constraint(weights, pltpu.HBM)
    send, becp = run_back(rows, slot_count, partials, mask, strength, window, weights, field)
    recv = to_all(send)
    return run_spectrum(recv, coefficients, kinetic), becp


def solution(mesh):
    in_specs = (
        P(None, None, "pencil", None), P("pencil", None, None), P("pencil"), P("pencil"),
        P("pencil", None), P("pencil", None, None), P(), P(),
    )
    out_specs = (P(None, None, "pencil", None), P("pencil", None))
    return jax.shard_map(per_device, mesh=mesh, in_specs=in_specs, out_specs=out_specs, check_vma=False)
```

```python
import jax
import jax.numpy as jnp
import ml_dtypes
import numpy as np
from jax import lax
from jax.experimental import pallas as pl
from jax.experimental.pallas import tpu as pltpu
from jax.sharding import PartitionSpec as P

GRID = 256
CUT = 128
NPROJ = 8
REACH = 2
BANDS = 8
SLOTS = 64
NPTS = 256
ROWS = 16384
WINDOW = 2 * REACH + 1
F32 = jnp.float32
BF16 = jnp.bfloat16
UNROLL = 8
BATCH = 16
CHUNK = 8
TO_GRID = CUT ** -1.5
TO_WAVES = GRID ** -1.5


def halves(table):
    table = np.asarray(table, np.float64)
    high = table.astype(np.float32).astype(ml_dtypes.bfloat16)
    low = (table - high.astype(np.float64)).astype(np.float32).astype(ml_dtypes.bfloat16)
    return high, low


def make_tables():
    freq = np.arange(CUT) - CUT // 2
    turns = (freq[:, None] * np.arange(GRID)[None, :]) % GRID
    cos = np.cos(2 * np.pi * turns / GRID)
    sin = np.sin(2 * np.pi * turns / GRID)
    forward = np.block([[cos, sin], [-sin, cos]])
    return dict(f=halves(forward), ft=halves(forward.T))


TABLES = make_tables()


def split(value):
    high = value.astype(BF16)
    low = (value - high.astype(F32)).astype(BF16)
    return high, low


def mm(a, b):
    return lax.dot_general(a, b, (((1,), (0,)), ((), ())), preferred_element_type=F32)


def mm_nt(a, b):
    return lax.dot_general(a, b, (((1,), (1,)), ((), ())), preferred_element_type=F32)


def mm_tn(a, b):
    return lax.dot_general(a, b, (((0,), (0,)), ((), ())), preferred_element_type=F32)


def mm_three(table_high, table_low, high, low):
    return mm(jnp.concatenate([table_high, table_low, table_high], 1), jnp.concatenate([high, high, low], 0))


def mm_three_right(high, low, table_high, table_low):
    return mm(jnp.concatenate([high, low, high], 1), jnp.concatenate([table_high, table_high, table_low], 0))


def lane_iota(shape):
    return lax.broadcasted_iota(jnp.int32, shape, len(shape) - 1)


def exchange_blocks(arrays):
    rows = arrays[0].shape[0]
    block = lane_iota((rows, 128)) // 8
    rolled = [pltpu.roll(a, 8 * i, 1) if i else a for i, a in enumerate(arrays)]
    vals = [rolled[(-n) % 16] for n in range(16)]
    for bit in range(4):
        step = 1 << bit
        chosen = (block // step) % 2 == 1
        vals = [jnp.where(chosen, vals[(j - step) % 16], vals[j]) for j in range(16)]
    return [pltpu.roll(v, (128 - 8 * j) % 128, 1) if j else v for j, v in enumerate(vals)]


def swap_parts(value, first_sign):
    sign = jnp.where(lane_iota(value.shape) < 64, first_sign, -first_sign)
    return pltpu.roll(value, 64, 1) * sign


def block_ones():
    row = lax.broadcasted_iota(jnp.int32, (128, 128), 0) // 8
    col = lax.broadcasted_iota(jnp.int32, (128, 128), 1) // 8
    return (row == col).astype(F32)


def three(value):
    a = value.astype(BF16)
    rest = value - a.astype(F32)
    b = rest.astype(BF16)
    c = (rest - b.astype(F32)).astype(BF16)
    return a, b, c


def exact_times_ones(value, ones):
    ones = ones.astype(BF16)
    a, b, c = three(value)
    return mm(a, ones) + mm(b, ones) + mm(c, ones)


def slot_weights(values, groups):
    return jnp.concatenate([jnp.where(groups == g, values, 0.0) for g in range(8)], 0)


def columns_kernel(coef_ref, th_ref, tl_ref, out_ref):
    th, tl = th_ref[...], tl_ref[...]
    for b in range(BANDS):
        a = jnp.concatenate([coef_ref[0, b], coef_ref[1, b]], 1)
        ah, al = split(a)
        res = mm_nt(jnp.concatenate([th, tl, th], 1), jnp.concatenate([ah, ah, al], 1))
        for o in range(2):
            out_ref[pl.ds(o * 8 + b, 256, stride=16), :] = TO_GRID * res[o * 256:(o + 1) * 256]


def slots_kernel(count_sm, value_ref, group_ref, rowf_ref, out_ref):
    near = lax.broadcasted_iota(jnp.int32, (128, 128), 0) // BATCH == lane_iota((128, 128)) // BATCH
    low_lane = lane_iota((128, 128)) < 64

    def one_slot(s):
        w = slot_weights(value_ref[s], group_ref[pl.ds(s, 1), :])
        wh, wl = split(w)
        both = jnp.concatenate([wh, wl], 0)
        all_rows = rowf_ref[pl.ds(s, 1), :]
        for h in range(2):
            cols = slice(h * 128, (h + 1) * 128)
            rows = jnp.broadcast_to(all_rows[:, cols], (128, 128))
            same = jnp.where((rows == rows.T) & near, 1.0, 0.0).astype(BF16)
            res = mm_nt(same, both[:, cols])
            total = res + pltpu.roll(res, 64, 1)
            high = total.astype(BF16).astype(F32)
            out_ref[s, cols, :] = jnp.where(low_lane, high, total - high).astype(BF16)

    def two_slots(i, carry):
        one_slot(i * 2)
        one_slot(i * 2 + 1)
        return carry

    lax.fori_loop(0, (count_sm[0] + 3) // 4 * 2, two_slots, 0)


def grid_kernel(
    rows_sm, count_sm,
    pot_hbm, value_hbm, recv_ref, group_ref, window_ref,
    yh_ref, yl_ref, th_ref, tl_ref,
    field_hbm, partial_ref,
    ah_s, al_s, ys_s, inha_s, inla_s, inhb_s, inlb_s, u_s, w_s, ga_s, gb_s, z_s, pot_ref, value_ref, sem, pot_sem, value_sem,
):
    pot_copy = pltpu.make_async_copy(pot_hbm, pot_ref, pot_sem)
    pot_copy.start()
    value_copy = pltpu.make_async_copy(value_hbm, value_ref, value_sem)
    value_copy.start()
    yh, yl = yh_ref[...], yl_ref[...]
    piece = lax.broadcasted_iota(jnp.int32, (32, 128), 0)
    pick_group = (lane_iota((32, 128)) % 8 == piece % 8).astype(F32).astype(BF16)
    def along_y(zz):
        for b in range(BANDS):
            for r in range(2):
                part = recv_ref[pl.ds(zz * 16 + r * 8 + b, 128, stride=32), :]
                h, l = split(part)
                ah_s[b * 128:(b + 1) * 128, r * 128:(r + 1) * 128] = h
                al_s[b * 128:(b + 1) * 128, r * 128:(r + 1) * 128] = l
        ys_s[zz] = mm_three_right(ah_s[...], al_s[...], yh, yl)

    along_y(0)

    def permute(unit, kc):
        zz, half = unit // 2, unit % 2
        base = pl.multiple_of(kc * 16, 16)
        ins = [
            ys_s[zz, pl.ds((i % 8) * 128 + base, 16), ((i // 8) * 2 + half) * 128:((i // 8) * 2 + half + 1) * 128]
            for i in range(16)
        ]
        for j, v in enumerate(exchange_blocks(ins)):
            cols = slice((j % 2) * 128, (j % 2 + 1) * 128)
            vh, vl = split(v)
            sh, sl = split(swap_parts(v, -1.0))
            inh_s, inl_s = buffers[unit % 2]
            inh_s[j // 2, pl.ds(base, 16), cols] = vh
            inl_s[j // 2, pl.ds(base, 16), cols] = vl
            inh_s[j // 2, pl.ds(128 + base, 16), cols] = sh
            inl_s[j // 2, pl.ds(128 + base, 16), cols] = sl

    def along_x(unit, pair):
        zz, half = unit // 2, unit % 2
        inh_s, inl_s = buffers[unit % 2]
        xh = jnp.concatenate([th_ref[:256, :128], th_ref[256:, :128]], 1)
        xl = jnp.concatenate([tl_ref[:256, :128], tl_ref[256:, :128]], 1)
        res = mm_three(xh, xl, inh_s[pair], inl_s[pair])
        for k in range(2):
            yg = half * 16 + pair * 2 + k
            pot = pot_ref[zz, pl.ds(pl.multiple_of(yg * 8, 8), 8), :]
            pa, pb, pc = three(pot)
            pieces = jnp.concatenate([pa.astype(F32), pb.astype(F32), pc.astype(F32), jnp.zeros((8, 256), F32)], 0)
            spread = mm_tn(pieces.astype(BF16), pick_group)
            u = res[:, k * 128:(k + 1) * 128]
            at = pl.multiple_of((zz * 32 + yg) * 256, 256)
            u_s[pl.ds(at, 256), :] = u
            w_s[pl.ds(at, 256), :] = u * spread

    buffers = ((inha_s, inla_s), (inhb_s, inlb_s))
    for unit in range(-1, 4):
        if unit == 0:
            pot_copy.wait()
            along_y(1)

        def step(i, carry, unit=unit):
            if unit >= 0:
                along_x(unit, i)
            if unit < 3:
                permute(unit + 1, i)
            return carry

        lax.fori_loop(0, 8, step, 0, unroll=UNROLL)
    out_copy = pltpu.make_async_copy(w_s, field_hbm, sem)
    out_copy.start()
    z_s[...] = jnp.zeros((SLOTS * 8, 128), F32)
    own = lane_iota((64, 128)) % 8 == lax.broadcasted_iota(jnp.int32, (64, 128), 0) // 8

    count = count_sm[0]

    def pick(s, buf):
        for c in range(0, NPTS, 16):
            vals = [u_s[pl.ds(rows_sm[s * NPTS + c + k], 1), :] for k in range(16)]
            for k in range(16):
                buf[c + k:c + k + 1, :] = vals[k]

    def reduce_slot(s, buf):
        gh, gl = split(buf[...])
        w = slot_weights(value_ref[s], group_ref[pl.ds(s, 1), :])
        wh, wl = split(w)
        prod = mm(jnp.concatenate([wh, wl], 0), jnp.concatenate([gh, gl], 1))
        total = prod[:64, :128] + prod[64:, :128] + prod[:64, 128:]
        total = jnp.where(own, total, 0.0)
        z = total[0:8]
        for g in range(1, 8):
            z = z + total[g * 8:(g + 1) * 8]
        z_s[pl.ds(pl.multiple_of(s * 8, 8), 8), :] = jnp.where(s < count, z, 0.0)

    def two_slots(i, carry):
        s = i * 2
        pick(s + 1, gb_s)
        reduce_slot(s, ga_s)
        pick(jnp.minimum(s + 2, SLOTS - 1), ga_s)
        reduce_slot(s + 1, gb_s)
        return carry

    value_copy.wait()
    pick(0, ga_s)
    lax.fori_loop(0, (count + 1) // 2, two_slots, 0)
    spread = exact_times_ones(z_s[...], block_ones())
    mine = lane_iota((512, 128)) % 8 == lax.broadcasted_iota(jnp.int32, (512, 128), 0) % 8
    slot_terms = jnp.sum(jnp.where(mine, spread, 0.0).reshape(SLOTS, 8, 128), 1)
    onehot = (lax.broadcasted_iota(jnp.int32, (WINDOW * 16, SLOTS), 0) == window_ref[...]).astype(F32).astype(BF16)
    a, b, c = three(slot_terms)
    partial_ref[...] = mm(onehot, a) + mm(onehot, b) + mm(onehot, c)
    out_copy.wait()


def back_kernel(
    rows_sm, count_sm,
    near_ref, after_ref, before_ref,
    mask_ref, strength_ref, window_ref,
    yh_ref, yl_ref,
    weight_hbm, field_hbm,
    out_ref, becp_ref,
    w_s, weight_ref, tot_s, f_s, ta_s, tb_s, tc_s, td_s, xa_s, xb_s, ah_s, al_s, sem, chunk_sem,
):
    def chunk_copy(c):
        part = pl.ds(c * CHUNK, CHUNK)
        return pltpu.make_async_copy(weight_hbm.at[part], weight_ref.at[part], chunk_sem.at[c])

    chunk_copy(0).start()
    field_copy = pltpu.make_async_copy(field_hbm, w_s, sem)
    field_copy.start()
    for c in range(1, SLOTS // CHUNK):
        chunk_copy(c).start()

    tot_s[...] = near_ref[16:96]
    tot_s[32:] = tot_s[32:] + after_ref[...]
    tot_s[:48] = tot_s[:48] + before_ref[...]
    becp = jnp.where(mask_ref[...] > 0.0, tot_s[...], 0.0)
    becp_ref[...] = becp[REACH * 16:(REACH + 1) * 16]
    energy = becp * strength_ref[...]
    onehot = (lax.broadcasted_iota(jnp.int32, (WINDOW * 16, SLOTS), 0) == window_ref[...]).astype(F32).astype(BF16)
    a, b, c = three(energy)
    slot_energy = mm_tn(onehot, a) + mm_tn(onehot, b) + mm_tn(onehot, c)
    mine = lane_iota((512, 128)) % 8 == lax.broadcasted_iota(jnp.int32, (512, 128), 0) % 8
    wide = jnp.broadcast_to(slot_energy[:, None, :], (SLOTS, 8, 128)).reshape(SLOTS * 8, 128)
    f_s[...] = exact_times_ones(jnp.where(mine, wide, 0.0), block_ones())
    own = lane_iota((64, 128)) % 8 == lax.broadcasted_iota(jnp.int32, (64, 128), 0) // 8
    count = count_sm[0]

    def terms_of(s, buf):
        f = f_s[pl.ds(pl.multiple_of(s * 8, 8), 8), :]
        f = jnp.where(s < count, f, 0.0)
        diag = jnp.where(own, jnp.concatenate([f] * 8, 0), 0.0)
        pieces = jnp.concatenate(split(diag), 1)
        both = mm(weight_ref[s], jnp.concatenate([pieces, pieces], 0))
        buf[...] = both[:, :128] + both[:, 128:]

    def add_two(s, first, second):
        for buf, slot in ((first, s), (second, s + 1)):
            for c in range(0, NPTS, BATCH):
                at = [rows_sm[slot * NPTS + c + k] for k in range(BATCH)]
                vals = [w_s[pl.ds(at[k], 1), :] + buf[c + k:c + k + 1, :] for k in range(BATCH)]
                for k in range(BATCH):
                    w_s[pl.ds(at[k], 1), :] = vals[k]

    def four_slots(i, carry):
        s = i * 4
        later = jnp.minimum(s + 4, SLOTS - 2)

        @pl.when((lax.rem(i, 2) == 1) & (s + 4 < SLOTS))
        def _():
            chunk_copy((s + 4) // CHUNK).wait()

        terms_of(s + 2, tc_s)
        terms_of(s + 3, td_s)
        add_two(s, ta_s, tb_s)
        terms_of(later, ta_s)
        terms_of(later + 1, tb_s)
        add_two(s + 2, tc_s, td_s)
        return carry

    fours = (count + 3) // 4
    chunk_copy(0).wait()
    terms_of(0, ta_s)
    terms_of(1, tb_s)
    field_copy.wait()
    lax.fori_loop(0, fours, four_slots, 0)

    def drain(c, carry):
        chunk_copy(c).wait()
        return carry

    lax.fori_loop(jnp.minimum(fours // 2, SLOTS // CHUNK - 1) + 1, SLOTS // CHUNK, drain, 0)

    def along_x(unit, pair):
        zz, half = unit // 2, unit % 2
        at = pl.multiple_of((zz * 32 + half * 16 + pair * 2) * 256, 256)
        h0, l0 = split(w_s[pl.ds(at, 256), :])
        h1, l1 = split(w_s[pl.ds(at + 256, 256), :])
        bh, bl = jnp.concatenate([h0, h1], 1), jnp.concatenate([l0, l1], 1)
        xh = jnp.concatenate([yh_ref[:128, :256], yh_ref[:128, 256:]], 0)
        xl = jnp.concatenate([yl_ref[:128, :256], yl_ref[:128, 256:]], 0)
        res = mm_three(xh, xl, bh, bl)
        for k in range(2):
            cols = slice(k * 128, (k + 1) * 128)
            buffers[unit % 2][pair * 2 + k] = res[:128, cols] + swap_parts(res[128:, cols], 1.0)

    def permute(unit, kc):
        half = unit % 2
        base = pl.multiple_of(kc * 16, 16)
        ins = [buffers[unit % 2][j, pl.ds(base, 16), :] for j in range(16)]
        for i, v in enumerate(exchange_blocks(ins)):
            vh, vl = split(v)
            lo = ((i // 8) * 2 + half) * 128
            ah_s[pl.ds((i % 8) * 128 + base, 16), lo:lo + 128] = vh
            al_s[pl.ds((i % 8) * 128 + base, 16), lo:lo + 128] = vl

    buffers = (xa_s, xb_s)
    for unit in range(-1, 4):
        def step(i, carry, unit=unit):
            if unit < 3:
                along_x(unit + 1, i)
            if unit >= 0:
                permute(unit, i)
            return carry

        lax.fori_loop(0, 8, step, 0, unroll=UNROLL)
        if unit in (1, 3):
            zz = unit // 2
            yh, yl = yh_ref[...], yl_ref[...]
            ah, al = ah_s[...], al_s[...]
            res = mm_nt(jnp.concatenate([ah, al, ah], 1), jnp.concatenate([yh, yh, yl], 1))
            for b in range(BANDS):
                for o in range(2):
                    part = res[b * 128:(b + 1) * 128, o * 128:(o + 1) * 128]
                    out_ref[pl.ds(zz * 16 + o * 8 + b, 128, stride=32), :] = part


def spectrum_kernel(recv_ref, coef_ref, kin_ref, th_ref, tl_ref, out_ref):
    th, tl = th_ref[...], tl_ref[...]
    kin = kin_ref[...]
    for b in range(BANDS):
        parts = [recv_ref[pl.ds(o * 8 + b, 256, stride=16), :] for o in range(2)]
        ah, al = split(jnp.concatenate(parts, 0))
        res = mm_tn(jnp.concatenate([ah, al, ah], 0), jnp.concatenate([th, th, tl], 0))
        for o in range(2):
            out_ref[o, b] = TO_WAVES * res[:, o * 128:(o + 1) * 128] + kin * coef_ref[o, b]


VM = pl.BlockSpec(memory_space=pltpu.VMEM)
HBM = pl.BlockSpec(memory_space=pltpu.HBM)
SM = pl.BlockSpec(memory_space=pltpu.SMEM)
SEND = pltpu.VMEM((4096, 128), F32)


def params(mebibytes):
    return pltpu.CompilerParams(vmem_limit_bytes=mebibytes * 1024 * 1024)


def run_columns(coef):
    return pl.pallas_call(
        columns_kernel,
        out_shape=jax.ShapeDtypeStruct((4096, 128), F32),
        in_specs=[VM] * 3, out_specs=VM, compiler_params=params(56), name="columns",
    )(coef, *TABLES["ft"])


def run_grid(rows, count, recv, pot, value, group, window):
    return pl.pallas_call(
        grid_kernel,
        out_shape=(pltpu.HBM((ROWS, 128), F32), pltpu.VMEM((WINDOW * 16, 128), F32)),
        in_specs=[SM, SM, HBM, HBM] + [VM] * 7,
        out_specs=(HBM, VM),
        scratch_shapes=[
            pltpu.VMEM((1024, 256), BF16), pltpu.VMEM((1024, 256), BF16),
            pltpu.VMEM((2, 1024, 512), F32),
            pltpu.VMEM((8, 256, 256), BF16), pltpu.VMEM((8, 256, 256), BF16),
            pltpu.VMEM((8, 256, 256), BF16), pltpu.VMEM((8, 256, 256), BF16),
            pltpu.VMEM((ROWS, 128), F32), pltpu.VMEM((ROWS, 128), F32),
            pltpu.VMEM((NPTS, 128), F32), pltpu.VMEM((NPTS, 128), F32), pltpu.VMEM((SLOTS * 8, 128), F32),
            pltpu.VMEM((2, GRID, GRID), F32), pltpu.VMEM((SLOTS, NPROJ, NPTS), F32),
            pltpu.SemaphoreType.DMA(()), pltpu.SemaphoreType.DMA(()), pltpu.SemaphoreType.DMA(()),
        ],
        compiler_params=params(34), name="grid",
    )(rows, count, pot, value, recv, group, window, *TABLES["f"], *TABLES["ft"])


def run_slots(count, value, group, rowf):
    return pl.pallas_call(
        slots_kernel,
        out_shape=pltpu.HBM((SLOTS, NPTS, 128), BF16),
        in_specs=[SM] + [VM] * 3, out_specs=VM, compiler_params=params(16), name="slots",
        cost_estimate=pl.CostEstimate(flops=10 ** 10, transcendentals=0, bytes_accessed=5 * 10 ** 6),
    )(count, value, group, rowf)


def run_back(rows, count, partials, mask, strength, window, weights, field):
    return pl.pallas_call(
        back_kernel,
        out_shape=(SEND, jax.ShapeDtypeStruct((16, 128), F32)),
        in_specs=[SM, SM] + [VM] * 8 + [HBM, HBM],
        out_specs=(VM, VM),
        scratch_shapes=[
            pltpu.VMEM((ROWS, 128), F32), pltpu.VMEM((SLOTS, NPTS, 128), BF16),
            pltpu.VMEM((WINDOW * 16, 128), F32),
            pltpu.VMEM((SLOTS * 8, 128), F32),
            pltpu.VMEM((NPTS, 128), F32), pltpu.VMEM((NPTS, 128), F32),
            pltpu.VMEM((NPTS, 128), F32), pltpu.VMEM((NPTS, 128), F32),
            pltpu.VMEM((16, 128, 128), F32), pltpu.VMEM((16, 128, 128), F32),
            pltpu.VMEM((1024, 512), BF16), pltpu.VMEM((1024, 512), BF16),
            pltpu.SemaphoreType.DMA(()), pltpu.SemaphoreType.DMA((SLOTS // CHUNK,)),
        ],
        compiler_params=params(28), name="back",
    )(rows, count, *partials, mask, strength, window, *TABLES["f"], weights, field)


def run_spectrum(recv, coef, kin):
    return pl.pallas_call(
        spectrum_kernel,
        out_shape=jax.ShapeDtypeStruct((2, BANDS, 128, 128), F32),
        in_specs=[VM] * 5, out_specs=VM, compiler_params=params(16), name="spectrum",
    )(recv, coef, kin, *TABLES["ft"])


def to_all(block):
    block = block.reshape(128, 32, 128)
    block = lax.all_to_all(block, "pencil", split_axis=0, concat_axis=0, tiled=True)
    return pltpu.with_memory_space_constraint(block.reshape(4096, 128), pltpu.VMEM)


def from_offset(block, delta):
    n = lax.axis_size("pencil")
    return lax.ppermute(block, "pencil", [((i + delta) % n, i) for i in range(n)])


def per_device(coefficients, potential, slot_atom, slot_count, point_offset, proj_value, proj_strength, proj_count):
    device = lax.axis_index("pencil")
    n_dev = lax.axis_size("pencil")
    atom_dev = proj_strength.shape[0] // n_dev
    rows = (point_offset >> 11) * 256 + (point_offset & 255)
    group = (point_offset >> 8) & 7
    rowf = rows.astype(F32)
    rows = rows.reshape(-1)
    window = ((slot_atom // atom_dev - device + REACH) % n_dev) * atom_dev + slot_atom % atom_dev
    window = window[None, :]
    atoms = ((device - REACH) * atom_dev + jnp.arange(WINDOW * atom_dev, dtype=jnp.int32)) % (n_dev * atom_dev)
    strength = jnp.tile(proj_strength[atoms], (1, 16))
    mask = ((jnp.arange(128, dtype=jnp.int32) % NPROJ)[None, :] < proj_count[atoms][:, None]).astype(F32)
    freq = jnp.arange(CUT, dtype=jnp.int32) - CUT // 2
    freq_x = device - CUT // 2
    kinetic = 6.0 / (CUT * CUT) * ((freq_x * freq_x + freq * freq)[:, None] + (freq * freq)[None, :]).astype(F32)

    recv = to_all(run_columns(coefficients))
    weights = run_slots(slot_count, proj_value, group, rowf)
    prepared = (recv, rows, group, weights, window, strength, mask, kinetic)
    recv, rows, group, weights, window, strength, mask, kinetic = lax.optimization_barrier(prepared)
    in_hbm = [pltpu.with_memory_space_constraint(block, pltpu.HBM) for block in (potential, proj_value)]
    field, partial = run_grid(rows, slot_count, recv, *in_hbm, group, window)
    wide = jnp.pad(partial, ((16, 16), (0, 0)))
    wide = wide + jnp.pad(from_offset(partial, 1), ((32, 0), (0, 0))) + jnp.pad(from_offset(partial, -1), ((0, 32), (0, 0)))
    partials = (wide, from_offset(wide[:48], 3), from_offset(wide[64:], -3))
    partials = [pltpu.with_memory_space_constraint(block, pltpu.VMEM) for block in partials]
    field = pltpu.with_memory_space_constraint(field, pltpu.HBM)
    weights = pltpu.with_memory_space_constraint(weights, pltpu.HBM)
    send, becp = run_back(rows, slot_count, partials, mask, strength, window, weights, field)
    recv = to_all(send)
    return run_spectrum(recv, coefficients, kinetic), becp


def solution(mesh):
    in_specs = (
        P(None, None, "pencil", None), P("pencil", None, None), P("pencil"), P("pencil"),
        P("pencil", None), P("pencil", None, None), P(), P(),
    )
    out_specs = (P(None, None, "pencil", None), P("pencil", None))
    return jax.shard_map(per_device, mesh=mesh, in_specs=in_specs, out_specs=out_specs, check_vma=False)
```

```python
import jax
import jax.numpy as jnp
import ml_dtypes
import numpy as np
from jax import lax
from jax.experimental import pallas as pl
from jax.experimental.pallas import tpu as pltpu
from jax.sharding import PartitionSpec as P

GRID = 256
CUT = 128
NPROJ = 8
REACH = 2
BANDS = 8
SLOTS = 64
NPTS = 256
ROWS = 16384
WINDOW = 2 * REACH + 1
F32 = jnp.float32
BF16 = jnp.bfloat16
UNROLL = 8
BATCH = 16
CHUNK = 8
TO_GRID = CUT ** -1.5
TO_WAVES = GRID ** -1.5


def halves(table):
    table = np.asarray(table, np.float64)
    high = table.astype(np.float32).astype(ml_dtypes.bfloat16)
    low = (table - high.astype(np.float64)).astype(np.float32).astype(ml_dtypes.bfloat16)
    return high, low


def make_tables():
    freq = np.arange(CUT) - CUT // 2
    turns = (freq[:, None] * np.arange(GRID)[None, :]) % GRID
    cos = np.cos(2 * np.pi * turns / GRID)
    sin = np.sin(2 * np.pi * turns / GRID)
    forward = np.block([[cos, sin], [-sin, cos]])
    return dict(f=halves(forward), ft=halves(forward.T))


TABLES = make_tables()


def split(value):
    high = value.astype(BF16)
    low = (value - high.astype(F32)).astype(BF16)
    return high, low


def mm(a, b):
    return lax.dot_general(a, b, (((1,), (0,)), ((), ())), preferred_element_type=F32)


def mm_nt(a, b):
    return lax.dot_general(a, b, (((1,), (1,)), ((), ())), preferred_element_type=F32)


def mm_tn(a, b):
    return lax.dot_general(a, b, (((0,), (0,)), ((), ())), preferred_element_type=F32)


def mm_three(table_high, table_low, high, low):
    return mm(jnp.concatenate([table_high, table_low, table_high], 1), jnp.concatenate([high, high, low], 0))


def mm_three_right(high, low, table_high, table_low):
    return mm(jnp.concatenate([high, low, high], 1), jnp.concatenate([table_high, table_high, table_low], 0))


def lane_iota(shape):
    return lax.broadcasted_iota(jnp.int32, shape, len(shape) - 1)


def exchange_blocks(arrays):
    rows = arrays[0].shape[0]
    block = lane_iota((rows, 128)) // 8
    rolled = [pltpu.roll(a, 8 * i, 1) if i else a for i, a in enumerate(arrays)]
    vals = [rolled[(-n) % 16] for n in range(16)]
    for bit in range(4):
        step = 1 << bit
        chosen = (block // step) % 2 == 1
        vals = [jnp.where(chosen, vals[(j - step) % 16], vals[j]) for j in range(16)]
    return [pltpu.roll(v, (128 - 8 * j) % 128, 1) if j else v for j, v in enumerate(vals)]


def swap_parts(value, first_sign):
    sign = jnp.where(lane_iota(value.shape) < 64, first_sign, -first_sign)
    return pltpu.roll(value, 64, 1) * sign


def block_ones():
    row = lax.broadcasted_iota(jnp.int32, (128, 128), 0) // 8
    col = lax.broadcasted_iota(jnp.int32, (128, 128), 1) // 8
    return (row == col).astype(F32)


def three(value):
    a = value.astype(BF16)
    rest = value - a.astype(F32)
    b = rest.astype(BF16)
    c = (rest - b.astype(F32)).astype(BF16)
    return a, b, c


def exact_times_ones(value, ones):
    ones = ones.astype(BF16)
    a, b, c = three(value)
    return mm(a, ones) + mm(b, ones) + mm(c, ones)


def slot_weights(values, groups):
    return jnp.concatenate([jnp.where(groups == g, values, 0.0) for g in range(8)], 0)


def columns_kernel(coef_ref, th_ref, tl_ref, out_ref):
    th, tl = th_ref[...], tl_ref[...]
    for b in range(BANDS):
        a = jnp.concatenate([coef_ref[0, b], coef_ref[1, b]], 1)
        ah, al = split(a)
        res = mm_nt(jnp.concatenate([th, tl, th], 1), jnp.concatenate([ah, ah, al], 1))
        for o in range(2):
            out_ref[pl.ds(o * 8 + b, 256, stride=16), :] = TO_GRID * res[o * 256:(o + 1) * 256]


def slots_kernel(count_sm, value_ref, group_ref, rowf_ref, out_ref):
    near = lax.broadcasted_iota(jnp.int32, (128, 128), 0) // BATCH == lane_iota((128, 128)) // BATCH
    low_lane = lane_iota((128, 128)) < 64

    def one_slot(s):
        w = slot_weights(value_ref[s], group_ref[pl.ds(s, 1), :])
        wh, wl = split(w)
        both = jnp.concatenate([wh, wl], 0)
        all_rows = rowf_ref[pl.ds(s, 1), :]
        for h in range(2):
            cols = slice(h * 128, (h + 1) * 128)
            rows = jnp.broadcast_to(all_rows[:, cols], (128, 128))
            same = jnp.where((rows == rows.T) & near, 1.0, 0.0).astype(BF16)
            res = mm_nt(same, both[:, cols])
            total = res + pltpu.roll(res, 64, 1)
            high = total.astype(BF16).astype(F32)
            out_ref[s, cols, :] = jnp.where(low_lane, high, total - high).astype(BF16)

    def two_slots(i, carry):
        one_slot(i * 2)
        one_slot(i * 2 + 1)
        return carry

    lax.fori_loop(0, (count_sm[0] + 3) // 4 * 2, two_slots, 0)


def grid_kernel(
    rows_hbm, count_sm,
    pot_hbm, value_hbm, recv_ref, group_ref, window_ref,
    yh_ref, yl_ref, th_ref, tl_ref,
    field_hbm, partial_ref,
    ah_s, al_s, ys_s, inha_s, inla_s, inhb_s, inlb_s, u_s, w_s, ga_s, gb_s, z_s, pot_ref, value_ref, sem, pot_sem, value_sem, rows_sm, rows_sem,
):
    rows_copy = pltpu.make_async_copy(rows_hbm, rows_sm, rows_sem)
    rows_copy.start()
    pot_copy = pltpu.make_async_copy(pot_hbm, pot_ref, pot_sem)
    pot_copy.start()
    value_copy = pltpu.make_async_copy(value_hbm, value_ref, value_sem)
    value_copy.start()
    yh, yl = yh_ref[...], yl_ref[...]
    piece = lax.broadcasted_iota(jnp.int32, (32, 128), 0)
    pick_group = (lane_iota((32, 128)) % 8 == piece % 8).astype(F32).astype(BF16)
    def along_y(zz):
        for b in range(BANDS):
            for r in range(2):
                part = recv_ref[pl.ds(zz * 16 + r * 8 + b, 128, stride=32), :]
                h, l = split(part)
                ah_s[b * 128:(b + 1) * 128, r * 128:(r + 1) * 128] = h
                al_s[b * 128:(b + 1) * 128, r * 128:(r + 1) * 128] = l
        ys_s[zz] = mm_three_right(ah_s[...], al_s[...], yh, yl)

    along_y(0)

    def permute(unit, kc):
        zz, half = unit // 2, unit % 2
        base = pl.multiple_of(kc * 16, 16)
        ins = [
            ys_s[zz, pl.ds((i % 8) * 128 + base, 16), ((i // 8) * 2 + half) * 128:((i // 8) * 2 + half + 1) * 128]
            for i in range(16)
        ]
        for j, v in enumerate(exchange_blocks(ins)):
            cols = slice((j % 2) * 128, (j % 2 + 1) * 128)
            vh, vl = split(v)
            sh, sl = split(swap_parts(v, -1.0))
            inh_s, inl_s = buffers[unit % 2]
            inh_s[j // 2, pl.ds(base, 16), cols] = vh
            inl_s[j // 2, pl.ds(base, 16), cols] = vl
            inh_s[j // 2, pl.ds(128 + base, 16), cols] = sh
            inl_s[j // 2, pl.ds(128 + base, 16), cols] = sl

    def along_x(unit, pair):
        zz, half = unit // 2, unit % 2
        inh_s, inl_s = buffers[unit % 2]
        xh = jnp.concatenate([th_ref[:256, :128], th_ref[256:, :128]], 1)
        xl = jnp.concatenate([tl_ref[:256, :128], tl_ref[256:, :128]], 1)
        res = mm_three(xh, xl, inh_s[pair], inl_s[pair])
        for k in range(2):
            yg = half * 16 + pair * 2 + k
            pot = pot_ref[zz, pl.ds(pl.multiple_of(yg * 8, 8), 8), :]
            pa, pb, pc = three(pot)
            pieces = jnp.concatenate([pa.astype(F32), pb.astype(F32), pc.astype(F32), jnp.zeros((8, 256), F32)], 0)
            spread = mm_tn(pieces.astype(BF16), pick_group)
            u = res[:, k * 128:(k + 1) * 128]
            at = pl.multiple_of((zz * 32 + yg) * 256, 256)
            u_s[pl.ds(at, 256), :] = u
            w_s[pl.ds(at, 256), :] = u * spread

    buffers = ((inha_s, inla_s), (inhb_s, inlb_s))
    for unit in range(-1, 4):
        if unit == 0:
            pot_copy.wait()
            along_y(1)

        def step(i, carry, unit=unit):
            if unit >= 0:
                along_x(unit, i)
            if unit < 3:
                permute(unit + 1, i)
            return carry

        lax.fori_loop(0, 8, step, 0, unroll=UNROLL)
    out_copy = pltpu.make_async_copy(w_s, field_hbm, sem)
    out_copy.start()
    z_s[...] = jnp.zeros((SLOTS * 8, 128), F32)
    own = lane_iota((64, 128)) % 8 == lax.broadcasted_iota(jnp.int32, (64, 128), 0) // 8

    count = count_sm[0]

    def pick(s, buf):
        for c in range(0, NPTS, 16):
            vals = [u_s[pl.ds(rows_sm[s * NPTS + c + k], 1), :] for k in range(16)]
            for k in range(16):
                buf[c + k:c + k + 1, :] = vals[k]

    def reduce_slot(s, buf):
        gh, gl = split(buf[...])
        w = slot_weights(value_ref[s], group_ref[pl.ds(s, 1), :])
        wh, wl = split(w)
        prod = mm(jnp.concatenate([wh, wl], 0), jnp.concatenate([gh, gl], 1))
        total = prod[:64, :128] + prod[64:, :128] + prod[:64, 128:]
        total = jnp.where(own, total, 0.0)
        z = total[0:8]
        for g in range(1, 8):
            z = z + total[g * 8:(g + 1) * 8]
        z_s[pl.ds(pl.multiple_of(s * 8, 8), 8), :] = jnp.where(s < count, z, 0.0)

    def two_slots(i, carry):
        s = i * 2
        pick(s + 1, gb_s)
        reduce_slot(s, ga_s)
        pick(jnp.minimum(s + 2, SLOTS - 1), ga_s)
        reduce_slot(s + 1, gb_s)
        return carry

    value_copy.wait()
    rows_copy.wait()
    pick(0, ga_s)
    lax.fori_loop(0, (count + 1) // 2, two_slots, 0)
    spread = exact_times_ones(z_s[...], block_ones())
    mine = lane_iota((512, 128)) % 8 == lax.broadcasted_iota(jnp.int32, (512, 128), 0) % 8
    slot_terms = jnp.sum(jnp.where(mine, spread, 0.0).reshape(SLOTS, 8, 128), 1)
    onehot = (lax.broadcasted_iota(jnp.int32, (WINDOW * 16, SLOTS), 0) == window_ref[...]).astype(F32).astype(BF16)
    a, b, c = three(slot_terms)
    partial_ref[...] = mm(onehot, a) + mm(onehot, b) + mm(onehot, c)
    out_copy.wait()


def back_kernel(
    rows_hbm, count_sm,
    near_ref, after_ref, before_ref,
    mask_ref, strength_ref, window_ref,
    yh_ref, yl_ref,
    weight_hbm, field_hbm,
    out_ref, becp_ref,
    w_s, weight_ref, tot_s, f_s, ta_s, tb_s, tc_s, td_s, xa_s, xb_s, ah_s, al_s, sem, chunk_sem, rows_sm, rows_sem,
):
    rows_copy = pltpu.make_async_copy(rows_hbm, rows_sm, rows_sem)
    rows_copy.start()
    def chunk_copy(c):
        part = pl.ds(c * CHUNK, CHUNK)
        return pltpu.make_async_copy(weight_hbm.at[part], weight_ref.at[part], chunk_sem.at[c])

    chunk_copy(0).start()
    field_copy = pltpu.make_async_copy(field_hbm, w_s, sem)
    field_copy.start()
    for c in range(1, SLOTS // CHUNK):
        chunk_copy(c).start()

    tot_s[...] = near_ref[16:96]
    tot_s[32:] = tot_s[32:] + after_ref[...]
    tot_s[:48] = tot_s[:48] + before_ref[...]
    becp = jnp.where(mask_ref[...] > 0.0, tot_s[...], 0.0)
    becp_ref[...] = becp[REACH * 16:(REACH + 1) * 16]
    energy = becp * strength_ref[...]
    onehot = (lax.broadcasted_iota(jnp.int32, (WINDOW * 16, SLOTS), 0) == window_ref[...]).astype(F32).astype(BF16)
    a, b, c = three(energy)
    slot_energy = mm_tn(onehot, a) + mm_tn(onehot, b) + mm_tn(onehot, c)
    mine = lane_iota((512, 128)) % 8 == lax.broadcasted_iota(jnp.int32, (512, 128), 0) % 8
    wide = jnp.broadcast_to(slot_energy[:, None, :], (SLOTS, 8, 128)).reshape(SLOTS * 8, 128)
    f_s[...] = exact_times_ones(jnp.where(mine, wide, 0.0), block_ones())
    own = lane_iota((64, 128)) % 8 == lax.broadcasted_iota(jnp.int32, (64, 128), 0) // 8
    count = count_sm[0]

    def terms_of(s, buf):
        f = f_s[pl.ds(pl.multiple_of(s * 8, 8), 8), :]
        f = jnp.where(s < count, f, 0.0)
        diag = jnp.where(own, jnp.concatenate([f] * 8, 0), 0.0)
        pieces = jnp.concatenate(split(diag), 1)
        both = mm(weight_ref[s], jnp.concatenate([pieces, pieces], 0))
        buf[...] = both[:, :128] + both[:, 128:]

    def add_two(s, first, second):
        for buf, slot in ((first, s), (second, s + 1)):
            for c in range(0, NPTS, BATCH):
                at = [rows_sm[slot * NPTS + c + k] for k in range(BATCH)]
                vals = [w_s[pl.ds(at[k], 1), :] + buf[c + k:c + k + 1, :] for k in range(BATCH)]
                for k in range(BATCH):
                    w_s[pl.ds(at[k], 1), :] = vals[k]

    def four_slots(i, carry):
        s = i * 4
        later = jnp.minimum(s + 4, SLOTS - 2)

        @pl.when((lax.rem(i, 2) == 1) & (s + 4 < SLOTS))
        def _():
            chunk_copy((s + 4) // CHUNK).wait()

        terms_of(s + 2, tc_s)
        terms_of(s + 3, td_s)
        add_two(s, ta_s, tb_s)
        terms_of(later, ta_s)
        terms_of(later + 1, tb_s)
        add_two(s + 2, tc_s, td_s)
        return carry

    fours = (count + 3) // 4
    chunk_copy(0).wait()
    terms_of(0, ta_s)
    terms_of(1, tb_s)
    field_copy.wait()
    rows_copy.wait()
    lax.fori_loop(0, fours, four_slots, 0)

    def drain(c, carry):
        chunk_copy(c).wait()
        return carry

    lax.fori_loop(jnp.minimum(fours // 2, SLOTS // CHUNK - 1) + 1, SLOTS // CHUNK, drain, 0)

    def along_x(unit, pair):
        zz, half = unit // 2, unit % 2
        at = pl.multiple_of((zz * 32 + half * 16 + pair * 2) * 256, 256)
        h0, l0 = split(w_s[pl.ds(at, 256), :])
        h1, l1 = split(w_s[pl.ds(at + 256, 256), :])
        bh, bl = jnp.concatenate([h0, h1], 1), jnp.concatenate([l0, l1], 1)
        xh = jnp.concatenate([yh_ref[:128, :256], yh_ref[:128, 256:]], 0)
        xl = jnp.concatenate([yl_ref[:128, :256], yl_ref[:128, 256:]], 0)
        res = mm_three(xh, xl, bh, bl)
        for k in range(2):
            cols = slice(k * 128, (k + 1) * 128)
            buffers[unit % 2][pair * 2 + k] = res[:128, cols] + swap_parts(res[128:, cols], 1.0)

    def permute(unit, kc):
        half = unit % 2
        base = pl.multiple_of(kc * 16, 16)
        ins = [buffers[unit % 2][j, pl.ds(base, 16), :] for j in range(16)]
        for i, v in enumerate(exchange_blocks(ins)):
            vh, vl = split(v)
            lo = ((i // 8) * 2 + half) * 128
            ah_s[pl.ds((i % 8) * 128 + base, 16), lo:lo + 128] = vh
            al_s[pl.ds((i % 8) * 128 + base, 16), lo:lo + 128] = vl

    buffers = (xa_s, xb_s)
    for unit in range(-1, 4):
        def step(i, carry, unit=unit):
            if unit < 3:
                along_x(unit + 1, i)
            if unit >= 0:
                permute(unit, i)
            return carry

        lax.fori_loop(0, 8, step, 0, unroll=UNROLL)
        if unit in (1, 3):
            zz = unit // 2
            yh, yl = yh_ref[...], yl_ref[...]
            ah, al = ah_s[...], al_s[...]
            res = mm_nt(jnp.concatenate([ah, al, ah], 1), jnp.concatenate([yh, yh, yl], 1))
            for b in range(BANDS):
                for o in range(2):
                    part = res[b * 128:(b + 1) * 128, o * 128:(o + 1) * 128]
                    out_ref[pl.ds(zz * 16 + o * 8 + b, 128, stride=32), :] = part


def spectrum_kernel(recv_ref, coef_ref, kin_ref, th_ref, tl_ref, out_ref):
    th, tl = th_ref[...], tl_ref[...]
    kin = kin_ref[...]
    for b in range(BANDS):
        parts = [recv_ref[pl.ds(o * 8 + b, 256, stride=16), :] for o in range(2)]
        ah, al = split(jnp.concatenate(parts, 0))
        res = mm_tn(jnp.concatenate([ah, al, ah], 0), jnp.concatenate([th, th, tl], 0))
        for o in range(2):
            out_ref[o, b] = TO_WAVES * res[:, o * 128:(o + 1) * 128] + kin * coef_ref[o, b]


VM = pl.BlockSpec(memory_space=pltpu.VMEM)
HBM = pl.BlockSpec(memory_space=pltpu.HBM)
SM = pl.BlockSpec(memory_space=pltpu.SMEM)
SEND = pltpu.VMEM((4096, 128), F32)


def params(mebibytes):
    return pltpu.CompilerParams(vmem_limit_bytes=mebibytes * 1024 * 1024)


def run_columns(coef):
    return pl.pallas_call(
        columns_kernel,
        out_shape=jax.ShapeDtypeStruct((4096, 128), F32),
        in_specs=[VM] * 3, out_specs=VM, compiler_params=params(56), name="columns",
    )(coef, *TABLES["ft"])


def run_grid(rows, count, recv, pot, value, group, window):
    return pl.pallas_call(
        grid_kernel,
        out_shape=(pltpu.HBM((ROWS, 128), F32), pltpu.VMEM((WINDOW * 16, 128), F32)),
        in_specs=[HBM, SM, HBM, HBM] + [VM] * 7,
        out_specs=(HBM, VM),
        scratch_shapes=[
            pltpu.VMEM((1024, 256), BF16), pltpu.VMEM((1024, 256), BF16),
            pltpu.VMEM((2, 1024, 512), F32),
            pltpu.VMEM((8, 256, 256), BF16), pltpu.VMEM((8, 256, 256), BF16),
            pltpu.VMEM((8, 256, 256), BF16), pltpu.VMEM((8, 256, 256), BF16),
            pltpu.VMEM((ROWS, 128), F32), pltpu.VMEM((ROWS, 128), F32),
            pltpu.VMEM((NPTS, 128), F32), pltpu.VMEM((NPTS, 128), F32), pltpu.VMEM((SLOTS * 8, 128), F32),
            pltpu.VMEM((2, GRID, GRID), F32), pltpu.VMEM((SLOTS, NPROJ, NPTS), F32),
            pltpu.SemaphoreType.DMA(()), pltpu.SemaphoreType.DMA(()), pltpu.SemaphoreType.DMA(()),
            pltpu.SMEM((SLOTS * NPTS,), jnp.int32), pltpu.SemaphoreType.DMA(()),
        ],
        compiler_params=params(34), name="grid",
    )(rows, count, pot, value, recv, group, window, *TABLES["f"], *TABLES["ft"])


def run_slots(count, value, group, rowf):
    return pl.pallas_call(
        slots_kernel,
        out_shape=pltpu.HBM((SLOTS, NPTS, 128), BF16),
        in_specs=[SM] + [VM] * 3, out_specs=VM, compiler_params=params(16), name="slots",
        cost_estimate=pl.CostEstimate(flops=10 ** 10, transcendentals=0, bytes_accessed=5 * 10 ** 6),
    )(count, value, group, rowf)


def run_back(rows, count, partials, mask, strength, window, weights, field):
    return pl.pallas_call(
        back_kernel,
        out_shape=(SEND, jax.ShapeDtypeStruct((16, 128), F32)),
        in_specs=[HBM, SM] + [VM] * 8 + [HBM, HBM],
        out_specs=(VM, VM),
        scratch_shapes=[
            pltpu.VMEM((ROWS, 128), F32), pltpu.VMEM((SLOTS, NPTS, 128), BF16),
            pltpu.VMEM((WINDOW * 16, 128), F32),
            pltpu.VMEM((SLOTS * 8, 128), F32),
            pltpu.VMEM((NPTS, 128), F32), pltpu.VMEM((NPTS, 128), F32),
            pltpu.VMEM((NPTS, 128), F32), pltpu.VMEM((NPTS, 128), F32),
            pltpu.VMEM((16, 128, 128), F32), pltpu.VMEM((16, 128, 128), F32),
            pltpu.VMEM((1024, 512), BF16), pltpu.VMEM((1024, 512), BF16),
            pltpu.SemaphoreType.DMA(()), pltpu.SemaphoreType.DMA((SLOTS // CHUNK,)),
            pltpu.SMEM((SLOTS * NPTS,), jnp.int32), pltpu.SemaphoreType.DMA(()),
        ],
        compiler_params=params(28), name="back",
    )(rows, count, *partials, mask, strength, window, *TABLES["f"], weights, field)


def run_spectrum(recv, coef, kin):
    return pl.pallas_call(
        spectrum_kernel,
        out_shape=jax.ShapeDtypeStruct((2, BANDS, 128, 128), F32),
        in_specs=[VM] * 5, out_specs=VM, compiler_params=params(16), name="spectrum",
    )(recv, coef, kin, *TABLES["ft"])


def to_all(block):
    block = block.reshape(128, 32, 128)
    block = lax.all_to_all(block, "pencil", split_axis=0, concat_axis=0, tiled=True)
    return pltpu.with_memory_space_constraint(block.reshape(4096, 128), pltpu.VMEM)


def from_offset(block, delta):
    n = lax.axis_size("pencil")
    return lax.ppermute(block, "pencil", [((i + delta) % n, i) for i in range(n)])


def per_device(coefficients, potential, slot_atom, slot_count, point_offset, proj_value, proj_strength, proj_count):
    device = lax.axis_index("pencil")
    n_dev = lax.axis_size("pencil")
    atom_dev = proj_strength.shape[0] // n_dev
    rows = (point_offset >> 11) * 256 + (point_offset & 255)
    group = (point_offset >> 8) & 7
    rowf = rows.astype(F32)
    rows = rows.reshape(-1)
    window = ((slot_atom // atom_dev - device + REACH) % n_dev) * atom_dev + slot_atom % atom_dev
    window = window[None, :]
    atoms = ((device - REACH) * atom_dev + jnp.arange(WINDOW * atom_dev, dtype=jnp.int32)) % (n_dev * atom_dev)
    strength = jnp.tile(proj_strength[atoms], (1, 16))
    mask = ((jnp.arange(128, dtype=jnp.int32) % NPROJ)[None, :] < proj_count[atoms][:, None]).astype(F32)
    freq = jnp.arange(CUT, dtype=jnp.int32) - CUT // 2
    freq_x = device - CUT // 2
    kinetic = 6.0 / (CUT * CUT) * ((freq_x * freq_x + freq * freq)[:, None] + (freq * freq)[None, :]).astype(F32)

    recv = to_all(run_columns(coefficients))
    weights = run_slots(slot_count, proj_value, group, rowf)
    prepared = (recv, rows, group, weights, window, strength, mask, kinetic)
    recv, rows, group, weights, window, strength, mask, kinetic = lax.optimization_barrier(prepared)
    rows = pltpu.with_memory_space_constraint(rows, pltpu.HBM)
    in_hbm = [pltpu.with_memory_space_constraint(block, pltpu.HBM) for block in (potential, proj_value)]
    field, partial = run_grid(rows, slot_count, recv, *in_hbm, group, window)
    wide = jnp.pad(partial, ((16, 16), (0, 0)))
    wide = wide + jnp.pad(from_offset(partial, 1), ((32, 0), (0, 0))) + jnp.pad(from_offset(partial, -1), ((0, 32), (0, 0)))
    partials = (wide, from_offset(wide[:48], 3), from_offset(wide[64:], -3))
    partials = [pltpu.with_memory_space_constraint(block, pltpu.VMEM) for block in partials]
    field = pltpu.with_memory_space_constraint(field, pltpu.HBM)
    weights = pltpu.with_memory_space_constraint(weights, pltpu.HBM)
    send, becp = run_back(rows, slot_count, partials, mask, strength, window, weights, field)
    recv = to_all(send)
    return run_spectrum(recv, coefficients, kinetic), becp


def solution(mesh):
    in_specs = (
        P(None, None, "pencil", None), P("pencil", None, None), P("pencil"), P("pencil"),
        P("pencil", None), P("pencil", None, None), P(), P(),
    )
    out_specs = (P(None, None, "pencil", None), P("pencil", None))
    return jax.shard_map(per_device, mesh=mesh, in_specs=in_specs, out_specs=out_specs, check_vma=False)
```
